32 devices in a mesh: users: 8 (over z, core), items: 4 (over y, x).
Axes of the slice: x: 2, y: 2, z: 4, core: 2. Of those that a mesh axis runs over, the one named last changes fastest.
Arguments:
- prefs: int32 [8192, 4096], P('users', 'items'), may hold values from 0 to 4
- item_weight: float32 [4096], P('items'), may hold values from 0.05 to 1.35
- clip_units: int32 [8192], P('users'), may hold values from 100 to 999
- user_emb: float32 [8192, 128], P(('users', 'items')), may hold values from -0.6 to 0.6
- user_acc: float32 [8192, 128], P(('users', 'items')), may hold values from 100 to 3000
- item_emb: float32 [4096, 128], P(('items', 'users')), may hold values from -0.6 to 0.6
- item_acc: float32 [4096, 128], P(('items', 'users')), may hold values from 100 to 3000
- noise: int32 [4096, 128], P(('items', 'users')), may hold values from -1000 to 1000
Outputs:
- new_user_emb: float32 [8192, 128], P(('users', 'items'))
- new_user_acc: float32 [8192, 128], P(('users', 'items'))
- new_item_emb: float32 [4096, 128], P(('items', 'users'))
- new_item_acc: float32 [4096, 128], P(('items', 'users'))
The draws below stay inside these ranges and needn't reach their ends.
All inputs are finite; a program needn't handle non-finite values.
Results may differ from the reference program's by a relative error of at most 0.0003.
Values sent between devices are 32-bit elements; how exact they have to be, the bound alone decides.
A program may use at most 64 MiB of HBM per device.

```python
import math
import jax
import jax.numpy as jnp
from jax import lax

K = 128
UD = 1024
NU = 8192
NI = 4096
N_USERS = 8


def draw_item_weight(key, part):
    position = jnp.arange(NI, dtype=jnp.float32) / NI
    base_rate = 0.1 * jnp.exp(jnp.log(9.0) * position)
    jitter = jax.random.uniform(key, (NI,), jnp.float32, 0.7, 1.3)
    return (base_rate * jitter).astype(jnp.float32)


def set_ends(drawn, key, least, top_value):
    shape = drawn.shape
    place = [jax.random.randint(jax.random.fold_in(key, axis), (), 0, shape[axis]) for axis in range(len(shape))]
    drawn = drawn.at[tuple(place)].set(least)
    longest = shape.index(max(shape))
    place[longest] = (place[longest] + 1) % shape[longest]
    return drawn.at[tuple(place)].set(top_value)


def shard_levels(stream_key, extent, cuts, low, high):
    level, own = 1.0, jax.random.fold_in(stream_key, 6)
    for dim, shards_of in cuts:
        steps = jnp.exp(jax.random.uniform(jax.random.fold_in(own, dim), (shards_of,), jnp.float32, low / len(cuts), high / len(cuts)))
        level = level * jnp.repeat(steps, extent[dim] // shards_of).reshape([-1 if axis == dim else 1 for axis in range(len(extent))])
    return level


def centred(rng, shape, spread, reach, shards=(), kind=jnp.bfloat16):
    level = shard_levels(rng, shape, shards, -0.22, 0.18) if shards else 1.0
    values = jax.random.normal(rng, shape, jnp.float32) * spread * level
    return jnp.minimum(jnp.maximum(values, -reach), reach).astype(kind)


def setup_inputs(seed: int = 0) -> dict:
    key_list = jax.random.split(jax.random.key(seed), 9)
    prefs = set_ends(jax.random.randint(key_list[0], (NU, NI), 0, 5), jax.random.fold_in(key_list[0], 1), 0, 4).astype(jnp.int32)
    item_weight = draw_item_weight(jax.random.fold_in(key_list[8], 71), 0)
    clip_units = set_ends(jax.random.randint(key_list[2], (NU,), 100, 1000), jax.random.fold_in(key_list[2], 1), 100, 999).astype(jnp.int32)
    user_emb = centred(key_list[3], (NU, K), 0.1, 0.6, ((0, 32),), jnp.float32)
    user_acc = jnp.clip(jnp.exp(math.log(3000.0) - 3.4011974 * jax.random.uniform(key_list[4], (NU, K), jnp.float32) ** shard_levels(key_list[4], (NU, K), ((0, 32),), -0.2, 0.2)), 100.0, 3000.0)
    item_emb = centred(key_list[5], (NI, K), 0.1, 0.6, ((0, 32),), jnp.float32)
    item_acc = jnp.clip(jnp.exp(math.log(3000.0) - 3.4011974 * jax.random.uniform(key_list[6], (NI, K), jnp.float32) ** shard_levels(key_list[6], (NI, K), ((0, 32),), -0.2, 0.2)), 100.0, 3000.0)
    noise = set_ends(jax.random.randint(key_list[7], (NI, K), -1000, 1001), jax.random.fold_in(key_list[7], 1), -1000, 1000).astype(jnp.int32)
    return {"prefs": prefs, "item_weight": item_weight, "clip_units": clip_units, "user_emb": user_emb, "user_acc": user_acc, "item_emb": item_emb, "item_acc": item_acc, "noise": noise}


noise_step = 0.05
learn_rate = 0.5

def reference(prefs, item_weight, clip_units, user_emb, user_acc, item_emb, item_acc, noise):
    precise = lax.Precision.HIGHEST
    pref_blocks = prefs.reshape(N_USERS, UD, NI)
    user_blocks = user_emb.reshape(N_USERS, UD, K)
    clip_blocks = clip_units.reshape(N_USERS, UD)
    bound_scale = 0.001 * jnp.sqrt(jnp.float32(NI * K))

    def visit(totals, inputs):
        pref_rows, user_rows, clip_rows = inputs
        predicted = lax.dot_general(user_rows, item_emb, (((1,), (1,)), ((), ())), precision=precise, preferred_element_type=jnp.float32)
        target = jnp.where(pref_rows > 0, 1.0, 0.0).astype(jnp.float32)
        confidence = 1.0 + item_weight[None, :] * pref_rows.astype(jnp.float32)
        weighted = -2.0 * confidence * (target - predicted)
        resid_sq = lax.optimization_barrier(jnp.sum(weighted * weighted, axis=1))
        user_sq = lax.optimization_barrier(jnp.sum(user_rows * user_rows, axis=1))
        factor = jnp.minimum(1.0, clip_rows.astype(jnp.float32) * bound_scale / jnp.sqrt(resid_sq * user_sq + 1e-06))
        gradient = jnp.dot(weighted, item_emb, precision=precise, preferred_element_type=jnp.float32)
        scaled = user_rows * factor[:, None]
        totals = totals + lax.dot_general(weighted, scaled, (((0,), (0,)), ((), ())), precision=precise, preferred_element_type=jnp.float32)
        return (totals, gradient)
    initial = jnp.zeros((NI, K), jnp.float32)
    item_sum, user_parts = lax.scan(visit, initial, (pref_blocks, user_blocks, clip_blocks))
    user_grad = user_parts.reshape(NU, K)
    item_grad = item_sum + noise_step * noise.astype(jnp.float32)
    new_user_acc = user_acc + user_grad * user_grad
    new_user_emb = user_emb - learn_rate * user_grad / jnp.sqrt(new_user_acc)
    new_item_acc = item_acc + item_grad * item_grad
    new_item_emb = item_emb - learn_rate * item_grad / jnp.sqrt(new_item_acc)
    return (new_user_emb, new_user_acc, new_item_emb, new_item_acc)
```

```python
import functools

import jax
import jax.numpy as jnp
from jax import lax
from jax.experimental import pallas as pl
from jax.experimental.pallas import tpu as pltpu
from jax.sharding import PartitionSpec as P

noise_step = 0.05
learn_rate = 0.5
MESH = pl.DeviceIdType.MESH
F32 = jnp.float32
BF16 = jnp.bfloat16


def split(x):
    high = x.astype(BF16)
    return high, (x - high.astype(F32)).astype(BF16)


def mm(a, b):
    return jnp.dot(a, b, preferred_element_type=F32)


def paired(here, relation):
    bit = 1
    while bit <= relation:
        if relation & bit:
            here = here + bit - 2 * bit * (here // bit % 2)
        bit *= 2
    return here


def line_kernel(
    prefs_hbm, weight_hbm, clip_hbm, user_hbm, item_hbm,
    user_grad_ref, item_sum_ref,
    prefs, weight_ref, clip_ref, users, items, conf, target, ucat, icat, users_t, w_high, w_low,
    sq, sq_part, grad, grad_in, part, pair_in, pair_sum, far_in, scat,
    load_sem, u_send, u_recv, z_send, z_recv, rl_send, rl_recv,
    sq_send, sq_recv, gr_send, gr_recv, pr_send, pr_recv, fr_send, fr_recv,
):
    ni, half = 4, 4
    me_u, me_i = lax.axis_index("users"), lax.axis_index("items")
    z, core = me_u // 2, me_u % 2
    inner = (z + 1) // 2 % 2
    partner = (2 * z + 1 - core, me_i)
    rows, cols = prefs.shape
    width = users.shape[1]
    ub, ib = rows // ni, cols // (2 * half)
    big, lane = 2 * ib, 128
    iq = ib // 2

    def zp(d):
        return paired(z, d)

    def by_role(at_end, between):
        return at_end + inner * (between - at_end)

    def u_at(d):
        return pl.multiple_of(paired(me_i, d) * ub, ub)

    def i_block(ref, to_z, of_core):
        return ref.at[pl.ds(pl.multiple_of((2 * to_z + of_core) * ib, ib), ib)]

    def item_peer(d):
        return (me_u, paired(me_i, d))

    def z_device(to_z):
        return (2 * to_z + core, me_i)

    load_i = pltpu.make_async_copy(item_hbm, i_block(items, z, core), load_sem.at[0])
    load_u = pltpu.make_async_copy(user_hbm, users.at[pl.ds(u_at(0), ub)], load_sem.at[1])
    load_p = pltpu.make_async_copy(prefs_hbm, prefs, load_sem.at[2])
    load_w = pltpu.make_async_copy(weight_hbm, weight_ref, load_sem.at[3])
    load_c = pltpu.make_async_copy(clip_hbm, clip_ref, load_sem.at[4])
    load_i.start()
    load_u.start()
    load_w.start()
    load_c.start()
    load_p.start()

    barrier = pltpu.get_barrier_semaphore()
    for d in (1, 2, 3):
        pl.semaphore_signal(barrier, inc=1, device_id=z_device(zp(d)), device_id_type=MESH)
        pl.semaphore_signal(barrier, inc=1, device_id=item_peer(d), device_id_type=MESH)
    pl.semaphore_signal(barrier, inc=1, device_id=partner, device_id_type=MESH)
    load_i.wait()
    load_u.wait()
    pl.semaphore_wait(barrier, 7)

    sent = []

    def remote(src, dst, send, recv, device):
        copy = pltpu.make_async_remote_copy(
            src_ref=src, dst_ref=dst, send_sem=send, recv_sem=recv,
            device_id=device, device_id_type=MESH,
        )
        sent.append(copy)
        return copy

    mine_i = i_block(items, z, core)
    mine_u = users.at[pl.ds(u_at(0), ub)]
    relays = [remote(mine_i, mine_i, rl_send.at[0], rl_recv.at[0], partner)]
    relays[0].start()
    z_copies, u_copies = {}, {}
    for d in (1, 3, 2):
        z_copies[d] = remote(mine_i, mine_i, z_send.at[d], z_recv.at[d], z_device(zp(d)))
        z_copies[d].start()
    for d in (1, 2, 3):
        u_copies[d] = remote(mine_u, mine_u, u_send.at[d], u_recv.at[d], item_peer(d))
        u_copies[d].start()

    def relay(d):
        z_copies[d].wait_recv()
        block = i_block(items, zp(d), core)
        relays.append(remote(block, block, rl_send.at[d], rl_recv.at[d], partner))
        relays[-1].start()

    def i_rows(d, of_core):
        return pl.ds(pl.multiple_of((2 * zp(d) + of_core) * ib, ib), ib)

    own, other = core, 1 - core

    def take_items(d, of_core):
        at = i_rows(d, of_core)
        high, low = split(items[at, :])
        icat[at, 0:width] = high
        icat[at, width : 2 * width] = low
        icat[at, 2 * width : 3 * width] = high

    def take_users(d):
        at = pl.ds(u_at(d), ub)
        high, low = split(users[at, :])
        ucat[at, 0:width] = high
        ucat[at, width : 2 * width] = high
        ucat[at, 2 * width : 3 * width] = low

    scored = set()

    def score(d, *blocks):
        at = pl.ds(u_at(d), ub)
        both = jnp.concatenate([icat[i_rows(*block), :] for block in blocks], axis=0)
        predicted = lax.dot_general(
            ucat[at, :], both, (((1,), (1,)), ((), ())), preferred_element_type=F32
        )
        total = sq_part[at, :] if d in scored else jnp.zeros((ub, lane), F32)
        scored.add(d)
        for n, block in enumerate(blocks):
            col = i_rows(*block)
            weighted = conf[at, col] * (predicted[:, n * ib : (n + 1) * ib] - target[at, col])
            high, low = split(weighted)
            w_high[at, col] = high
            w_low[at, col] = low
            total = total + weighted * weighted
        sq_part[at, :] = total

    load_w.wait()
    load_c.wait()
    load_p.wait()
    tile = 128

    @pl.loop(0, rows // tile)
    def _(t):
        at = pl.ds(pl.multiple_of(t * tile, tile), tile)
        level = prefs[at, :]
        conf[at, :] = 2.0 + (2.0 * weight_ref[...]) * level.astype(F32)
        target[at, :] = jnp.where(level > 0, 1.0, 0.0).astype(F32)

    take_users(0)
    take_items(0, own)
    relay(1)
    take_items(1, own)
    relays[0].wait_recv()
    relays[1].wait_recv()
    take_items(0, other)
    take_items(1, other)
    near = ((0, own), (0, other), (1, own), (1, other))
    far_own, far_other = ((2, own), (3, own)), ((2, other), (3, other))
    score(0, *near)
    for d in (1, 2):
        u_copies[d].wait_recv()
        take_users(d)
        score(d, *near)
    relay(2)
    relay(3)
    take_items(2, own)
    take_items(3, own)
    u_copies[3].wait_recv()
    take_users(3)
    score(3, *near)
    for d in (0, 1, 2, 3):
        score(d, *far_own)
    relays[2].wait_recv()
    relays[3].wait_recv()
    take_items(2, other)
    take_items(3, other)
    for d in (0, 1, 2, 3):
        score(d, *far_other)
    sq[0] = jnp.sum(sq_part[...].T, axis=0, keepdims=True)

    sq_copies = []
    for d in (3, 1, 2):
        sq_copies.append(remote(sq.at[0], sq.at[d], sq_send.at[d], sq_recv.at[d], item_peer(d)))
        sq_copies[-1].start()

    g_copies = []
    for d in (3, 1, 2, 0):
        at = pl.ds(u_at(d), ub)
        both = mm(w_high[at, :], icat[:, 0 : 2 * width])
        cross = mm(w_low[at, :], icat[:, 0:width])
        grad[at, :] = both[:, 0:width] + (both[:, width:] + cross)
        if d > 0:
            g_copies.append(
                remote(grad.at[at], grad_in.at[d - 1], gr_send.at[d], gr_recv.at[d], item_peer(d))
            )
            g_copies[-1].start()

    users_t[...] = users[...].T
    flat = users_t[...]
    user_sq = jnp.sum(flat * flat, axis=0, keepdims=True)
    for copy in sq_copies:
        copy.wait_recv()
    total_sq = sq[0]
    for d in (1, 2, 3):
        total_sq = total_sq + sq[d]
    bound_scale = 0.001 * jnp.sqrt(jnp.full((1, 1), float(cols * ni * width), F32))
    factor = jnp.minimum(
        1.0, clip_ref[...].astype(F32) * bound_scale / jnp.sqrt(total_sq * user_sq + 1e-06)
    )
    s_high, s_low = split(flat * factor)
    scat[0:width, :] = s_high
    scat[width:, :] = s_low

    pair_copies = {}

    def f_copy(k, c, src_z, to_z, slot):
        piece = pl.ds(c * iq, iq)
        return remote(
            pair_sum.at[src_z, piece], far_in.at[slot, piece],
            fr_send.at[k, c], fr_recv.at[slot, c], z_device(to_z),
        )

    def f_wait(slot, c):
        piece = far_in.at[slot, pl.ds(c * iq, iq)]
        pltpu.make_async_copy(piece, piece, fr_recv.at[slot, c]).wait()

    f_third = [f_copy(3, c, zp(3), zp(3), 3) for c in (0, 1)]

    def forward(d):
        to_z = zp(d)
        pair_copies[d].wait_recv()
        pair_sum[to_z] = i_block(part, to_z, core)[...] + pair_in[to_z]
        if d == 2:
            for c in (0, 1):
                f_copy(2, c, to_z, by_role(zp(1), zp(2)), 2).start()
        if d == 1:
            for c in (0, 1):
                f_copy(1, c, to_z, to_z, 1).start()
        if d == 3:

            @pl.when(inner == 0)
            def _():
                for c in (0, 1):
                    f_third[c].start()

    order = (2, 3, 1, 0)
    for n, d in enumerate(order):
        to_z = zp(d)
        col = pl.ds(pl.multiple_of(to_z * big, big), big)
        both = mm(scat[...], w_high[:, col])
        cross = mm(scat[0:width, :], w_low[:, col])
        part[col, :] = (both[0:width] + (both[width:] + cross)).T
        pair_copies[d] = remote(
            i_block(part, to_z, 1 - core), pair_in.at[to_z],
            pr_send.at[d], pr_recv.at[d], partner,
        )
        pair_copies[d].start()
        if n > 0:
            forward(order[n - 1])
    forward(0)

    @pl.when(inner == 1)
    def _():
        to_z = zp(3)
        for c in (0, 1):
            f_wait(2, c)
            piece = pl.ds(c * iq, iq)
            pair_sum[to_z, piece, :] = pair_sum[to_z, piece, :] + far_in[2, piece, :]
            f_third[c].start()

    for copy in g_copies:
        copy.wait_recv()
    user_grad = grad[pl.ds(u_at(0), ub), :]
    for d in (1, 2, 3):
        user_grad = user_grad + grad_in[d - 1]
    user_grad_ref[...] = user_grad

    for c in (0, 1):
        f_wait(1, c)
    item_sum_ref[...] = pair_sum[z] + far_in[1]

    @pl.when(inner == 0)
    def _():
        for c in (0, 1):
            f_wait(2, c)
        item_sum_ref[...] = item_sum_ref[...] + far_in[2]

    for copy in sent:
        copy.wait_send()
    for c in (0, 1):
        f_wait(3, c)
    item_sum_ref[...] = item_sum_ref[...] + far_in[3]


def step_kernel(
    nu, ni,
    prefs_hbm, weight_hbm, clip_hbm, user_hbm, item_hbm,
    user_grad_ref, item_sum_ref,
    prefs, weight_ref, clip_ref, users, items, conf, target, ucat, icat, users_t, w_high, w_low,
    sq, sq_part, grad, grad_in, part, pair_in, pair_sum, far_in, scat,
    load_sem, ug_send, ug_recv, ig_send, ig_recv, rl_send, rl_recv,
    sq_send, sq_recv, gr_send, gr_recv, pr_send, pr_recv, fr_send, fr_recv,
):
    me_u, me_i = lax.axis_index("users"), lax.axis_index("items")
    half = nu // 2
    z, core = me_u // 2, me_u % 2
    partner = (2 * z + 1 - core, me_i)
    rows, cols = prefs.shape
    width = users.shape[1]
    ub, ib = rows // ni, cols // nu

    def u_slot(owner):
        return users.at[pl.ds(pl.multiple_of(owner * ub, ub), ub)]

    def i_slot(ref, owner):
        return ref.at[pl.ds(pl.multiple_of(owner * ib, ib), ib)]

    def item_peer(d):
        return (me_u, paired(me_i, d))

    def z_peer(d):
        return (2 * paired(z, d) + core, me_i)

    load_i = pltpu.make_async_copy(item_hbm, i_slot(items, me_u), load_sem.at[0])
    load_u = pltpu.make_async_copy(user_hbm, u_slot(me_i), load_sem.at[1])
    load_p = pltpu.make_async_copy(prefs_hbm, prefs, load_sem.at[2])
    load_w = pltpu.make_async_copy(weight_hbm, weight_ref, load_sem.at[3])
    load_c = pltpu.make_async_copy(clip_hbm, clip_ref, load_sem.at[4])
    load_i.start()
    load_u.start()
    load_w.start()
    load_c.start()
    load_p.start()

    barrier = pltpu.get_barrier_semaphore()
    for d in range(1, half):
        pl.semaphore_signal(barrier, inc=1, device_id=z_peer(d), device_id_type=MESH)
    for d in range(1, ni):
        pl.semaphore_signal(barrier, inc=1, device_id=item_peer(d), device_id_type=MESH)
    pl.semaphore_signal(barrier, inc=1, device_id=partner, device_id_type=MESH)
    load_i.wait()
    load_u.wait()
    pl.semaphore_wait(barrier, half + ni - 1)

    def remote(src, dst, send, recv, device):
        return pltpu.make_async_remote_copy(
            src_ref=src, dst_ref=dst, send_sem=send, recv_sem=recv,
            device_id=device, device_id_type=MESH,
        )

    mine_i = i_slot(items, me_u)
    mine_u = u_slot(me_i)
    z_copies, relays, u_copies = [], [], []
    relays.append(remote(mine_i, mine_i, rl_send.at[0], rl_recv.at[0], partner))
    relays[0].start()
    for d in range(1, half):
        z_copies.append(remote(mine_i, mine_i, ig_send.at[d], ig_recv.at[d], z_peer(d)))
        z_copies[-1].start()
    for d in range(1, ni):
        u_copies.append(remote(mine_u, mine_u, ug_send.at[d], ug_recv.at[d], item_peer(d)))
        u_copies[-1].start()

    load_w.wait()
    load_c.wait()
    load_p.wait()
    tile = min(rows, 128)

    @pl.loop(0, rows // tile)
    def _(t):
        at = pl.ds(pl.multiple_of(t * tile, tile), tile)
        level = prefs[at, :]
        conf[at, :] = 2.0 + (2.0 * weight_ref[...]) * level.astype(F32)
        target[at, :] = jnp.where(level > 0, 1.0, 0.0).astype(F32)

    big, lane = 256, 128

    def relay(d):
        z_copies[d - 1].wait_recv()
        block = i_slot(items, 2 * paired(z, d) + core)
        relays.append(remote(block, block, rl_send.at[d], rl_recv.at[d], partner))
        relays[-1].start()

    def take_items(start, size):
        at = pl.ds(start, size)
        high, low = split(items[at, :])
        icat[at, 0:width] = high
        icat[at, width : 2 * width] = low
        icat[at, 2 * width : 3 * width] = high

    def take_users(start, size):
        at = pl.ds(start, size)
        high, low = split(users[at, :])
        ucat[at, 0:width] = high
        ucat[at, width : 2 * width] = high
        ucat[at, 2 * width : 3 * width] = low

    def score(row, height, start, extent, first):
        at = pl.ds(row, height)
        left = ucat[at, :]
        total = jnp.zeros((height, lane), F32) if first else sq_part[at, :]
        for k in range(extent // big):
            col = pl.ds(start + k * big, big)
            predicted = lax.dot_general(
                left, icat[col, :], (((1,), (1,)), ((), ())), preferred_element_type=F32
            )
            weighted = conf[at, col] * (predicted - target[at, col])
            high, low = split(weighted)
            w_high[at, col] = high
            w_low[at, col] = low
            square = weighted * weighted
            for m in range(big // lane):
                total = total + square[:, m * lane : (m + 1) * lane]
        sq_part[at, :] = total

    if half == 4 and ni == 4 and ub == big and cols == 4 * big:
        near = pl.multiple_of(z // 2 * (2 * big), 2 * big)

        def i_at(d):
            return pl.multiple_of(paired(z, d) * big, big)

        def u_at(d):
            return pl.multiple_of(paired(me_i, d) * ub, ub)

        relay(1)
        take_users(u_at(0), ub)
        relays[0].wait_recv()
        relays[1].wait_recv()
        take_items(near, 2 * big)
        score(u_at(0), ub, near, 2 * big, True)
        for d in (1, 2):
            u_copies[d - 1].wait_recv()
            take_users(u_at(d), ub)
            score(u_at(d), ub, near, 2 * big, True)
        relay(2)
        relay(3)
        u_copies[2].wait_recv()
        take_users(u_at(3), ub)
        score(u_at(3), ub, near, 2 * big, True)
        for d in (2, 3):
            relays[d].wait_recv()
            take_items(i_at(d), big)
            for t in range(ni):
                score(t * big, big, i_at(d), big, False)
        sq[0] = jnp.sum(sq_part[...].T, axis=0, keepdims=True)
    else:
        for d in range(1, half):
            relay(d)
        for copy in u_copies + relays:
            copy.wait_recv()
        take_items(0, cols)
        take_users(0, rows)

        @pl.loop(0, rows // big)
        def _(t):
            score(pl.multiple_of(t * big, big), big, 0, cols, True)

        sq[0] = jnp.sum(sq_part[...].T, axis=0, keepdims=True)

    sq_copies = []
    for d in range(1, ni):
        sq_copies.append(remote(sq.at[0], sq.at[d], sq_send.at[d], sq_recv.at[d], item_peer(d)))
        sq_copies[-1].start()

    g_copies = []
    for d in list(range(1, ni)) + [0]:
        owner = paired(me_i, d)
        at = pl.ds(pl.multiple_of(owner * ub, ub), ub)
        both = mm(w_high[at, :], icat[:, 0 : 2 * width])
        cross = mm(w_low[at, :], icat[:, 0:width])
        grad[at, :] = both[:, 0:width] + (both[:, width:] + cross)
        if d > 0:
            g_copies.append(
                remote(grad.at[at], grad_in.at[d - 1], gr_send.at[d], gr_recv.at[d], item_peer(d))
            )
            g_copies[-1].start()

    users_t[...] = users[...].T
    flat = users_t[...]
    user_sq = jnp.sum(flat * flat, axis=0, keepdims=True)
    for copy in sq_copies:
        copy.wait_recv()
    total_sq = sq[0]
    for d in range(1, ni):
        total_sq = total_sq + sq[d]
    bound_scale = 0.001 * jnp.sqrt(jnp.full((1, 1), float(cols * ni * width), F32))
    factor = jnp.minimum(
        1.0, clip_ref[...].astype(F32) * bound_scale / jnp.sqrt(total_sq * user_sq + 1e-06)
    )
    s_high, s_low = split(flat * factor)
    scat[0:width, :] = s_high
    scat[width:, :] = s_low

    chunk = max(2 * ib, min(256, cols))
    groups = cols // chunk
    per = half // groups
    my_group = z // per
    pair_copies, far_copies = {}, {}

    def relations(order):
        return [(groups - order) * per + e for e in range(per)]

    def forward(order):
        for d in relations(order):
            to_z = paired(z, d)
            pair_copies[d].wait_recv()
            pair_sum[to_z] = i_slot(part, 2 * to_z + core)[...] + pair_in[to_z]
            if d > 0:
                far_copies[d] = remote(
                    pair_sum.at[to_z], far_in.at[d], fr_send.at[d], fr_recv.at[d], z_peer(d)
                )
                far_copies[d].start()

    for order in range(1, groups + 1):
        group = paired(my_group, groups - order)
        col = pl.ds(pl.multiple_of(group * chunk, chunk), chunk)
        both = mm(scat[...], w_high[:, col])
        cross = mm(scat[0:width, :], w_low[:, col])
        part[col, :] = (both[0:width] + (both[width:] + cross)).T
        for d in relations(order):
            to_z = paired(z, d)
            pair_copies[d] = remote(
                i_slot(part, 2 * to_z + 1 - core), pair_in.at[to_z],
                pr_send.at[d], pr_recv.at[d], partner,
            )
            pair_copies[d].start()
        if order > 1:
            forward(order - 1)
    forward(groups)

    for copy in g_copies:
        copy.wait_recv()
    user_grad = grad[pl.ds(pl.multiple_of(me_i * ub, ub), ub), :]
    for d in range(1, ni):
        user_grad = user_grad + grad_in[d - 1]
    user_grad_ref[...] = user_grad

    sent = z_copies + relays + u_copies + sq_copies + g_copies + list(pair_copies.values())
    for copy in sent + list(far_copies.values()):
        copy.wait_send()
    item_sum = pair_sum[z]
    for d in range(1, half):
        far_copies[d].wait_recv()
        item_sum = item_sum + far_in[d]
    item_sum_ref[...] = item_sum


def update_kernel(
    user_grad, item_sum, user_emb, user_acc, item_emb, item_acc, noise,
    new_user_emb, new_user_acc, new_item_emb, new_item_acc,
):
    grad = user_grad[...]
    acc = user_acc[...] + grad * grad
    new_user_acc[...] = acc
    new_user_emb[...] = user_emb[...] - learn_rate * grad / jnp.sqrt(acc)
    grad = item_sum[...] + noise_step * noise[...].astype(F32)
    acc = item_acc[...] + grad * grad
    new_item_acc[...] = acc
    new_item_emb[...] = item_emb[...] - learn_rate * grad / jnp.sqrt(acc)


def local(prefs, item_weight, clip_units, user_emb, user_acc, item_emb, item_acc, noise):
    nu, ni = lax.axis_size("users"), lax.axis_size("items")
    rows, cols = prefs.shape
    ub, width = user_emb.shape
    ib = item_emb.shape[0]
    half = nu // 2
    vmem = pl.BlockSpec(memory_space=pltpu.VMEM)
    hbm = pl.BlockSpec(memory_space=pltpu.HBM)
    dma = pltpu.SemaphoreType.DMA
    line = nu == 8 and ni == 4 and ub == 256 and ib == 128 and width == 128
    if line:
        kernel = line_kernel
        semaphores = [
            dma((5,)),
            dma((4,)), dma((4,)),
            dma((4,)), dma((4,)),
            dma((4,)), dma((4,)),
            dma((4,)), dma((4,)),
            dma((4,)), dma((4,)),
            dma((4,)), dma((4,)),
            dma((4, 2)), dma((4, 2)),
        ]
    else:
        kernel = functools.partial(step_kernel, nu, ni)
        semaphores = [
            dma((5,)),
            dma((ni,)), dma((ni,)),
            dma((half,)), dma((half,)),
            dma((half,)), dma((half,)),
            dma((ni,)), dma((ni,)),
            dma((ni + 1,)), dma((ni + 1,)),
            dma((half,)), dma((half,)),
            dma((half,)), dma((half,)),
        ]
    user_grad, item_sum = pl.pallas_call(
        kernel,
        out_shape=(
            jax.ShapeDtypeStruct((ub, width), F32),
            jax.ShapeDtypeStruct((ib, width), F32),
        ),
        in_specs=[hbm] * 5,
        out_specs=(vmem, vmem),
        scratch_shapes=[
            pltpu.VMEM((rows, cols), jnp.int32),
            pltpu.VMEM((1, cols), F32),
            pltpu.VMEM((1, rows), jnp.int32),
            pltpu.VMEM((rows, width), F32),
            pltpu.VMEM((cols, width), F32),
            pltpu.VMEM((rows, cols), F32),
            pltpu.VMEM((rows, cols), F32),
            pltpu.VMEM((rows, 3 * width), BF16),
            pltpu.VMEM((cols, 3 * width), BF16),
            pltpu.VMEM((width, rows), F32),
            pltpu.VMEM((rows, cols), BF16),
            pltpu.VMEM((rows, cols), BF16),
            pltpu.VMEM((ni, 1, rows), F32),
            pltpu.VMEM((rows, 128), F32),
            pltpu.VMEM((rows, width), F32),
            pltpu.VMEM((ni - 1, ub, width), F32),
            pltpu.VMEM((cols, width), F32),
            pltpu.VMEM((half, ib, width), F32),
            pltpu.VMEM((half, ib, width), F32),
            pltpu.VMEM((half, ib, width), F32),
            pltpu.VMEM((2 * width, rows), BF16),
        ] + semaphores,
        compiler_params=pltpu.CompilerParams(
            collective_id=0, has_side_effects=True, vmem_limit_bytes=48 * 1024 * 1024
        ),
    )(*[pltpu.with_memory_space_constraint(x, pltpu.HBM) for x in (prefs, item_weight[None, :], clip_units[None, :], user_emb, item_emb)])
    user_shape = jax.ShapeDtypeStruct((ub, width), F32)
    item_shape = jax.ShapeDtypeStruct((ib, width), F32)
    vmem = pl.BlockSpec(memory_space=pltpu.VMEM)
    return pl.pallas_call(
        update_kernel,
        out_shape=(user_shape, user_shape, item_shape, item_shape),
        in_specs=[vmem] * 7,
        out_specs=(vmem,) * 4,
        compiler_params=pltpu.CompilerParams(vmem_limit_bytes=4 * 1024 * 1024),
    )(user_grad, item_sum, user_emb, user_acc, item_emb, item_acc, noise)


def solution(mesh):
    placed = (
        P("users", "items"),
        P("items"),
        P("users"),
        P(("users", "items"), None),
        P(("users", "items"), None),
        P(("items", "users"), None),
        P(("items", "users"), None),
        P(("items", "users"), None),
    )
    return jax.shard_map(
        local,
        mesh=mesh,
        in_specs=placed,
        out_specs=(
            P(("users", "items"), None),
            P(("users", "items"), None),
            P(("items", "users"), None),
            P(("items", "users"), None),
        ),
        check_vma=False,
    )
```

```python
import functools

import jax
import jax.numpy as jnp
from jax import lax
from jax.experimental import pallas as pl
from jax.experimental.pallas import tpu as pltpu
from jax.sharding import PartitionSpec as P

noise_step = 0.05
learn_rate = 0.5
MESH = pl.DeviceIdType.MESH
F32 = jnp.float32
BF16 = jnp.bfloat16


def split(x):
    high = x.astype(BF16)
    return high, (x - high.astype(F32)).astype(BF16)


def mm(a, b):
    return jnp.dot(a, b, preferred_element_type=F32)


def paired(here, relation):
    bit = 1
    while bit <= relation:
        if relation & bit:
            here = here + bit - 2 * bit * (here // bit % 2)
        bit *= 2
    return here


def line_kernel(
    prefs_hbm, weight_hbm, clip_hbm, user_hbm, item_hbm,
    user_grad_ref, item_sum_ref,
    prefs, weight_ref, clip_ref, users, items, conf, target, ucat, icat, users_t, w_high, w_low,
    sq, sq_part, grad, grad_in, part, pair_in, pair_sum, far_in, scat,
    load_sem, u_send, u_recv, z_send, z_recv, rl_send, rl_recv,
    sq_send, sq_recv, gr_send, gr_recv, pr_send, pr_recv, fr_send, fr_recv,
):
    ni, half = 4, 4
    me_u, me_i = lax.axis_index("users"), lax.axis_index("items")
    z, core = me_u // 2, me_u % 2
    inner = (z + 1) // 2 % 2
    partner = (2 * z + 1 - core, me_i)
    rows, cols = prefs.shape
    width = users.shape[1]
    ub, ib = rows // ni, cols // (2 * half)
    big, lane = 2 * ib, 128
    iq = ib // 2

    def zp(d):
        return paired(z, d)

    def by_role(at_end, between):
        return at_end + inner * (between - at_end)

    def u_at(d):
        return pl.multiple_of(paired(me_i, d) * ub, ub)

    def i_block(ref, to_z, of_core):
        return ref.at[pl.ds(pl.multiple_of((2 * to_z + of_core) * ib, ib), ib)]

    def item_peer(d):
        return (me_u, paired(me_i, d))

    def z_device(to_z):
        return (2 * to_z + core, me_i)

    load_i = pltpu.make_async_copy(item_hbm, i_block(items, z, core), load_sem.at[0])
    load_u = pltpu.make_async_copy(user_hbm, users.at[pl.ds(u_at(0), ub)], load_sem.at[1])
    load_p = pltpu.make_async_copy(prefs_hbm, prefs, load_sem.at[2])
    load_w = pltpu.make_async_copy(weight_hbm, weight_ref, load_sem.at[3])
    load_c = pltpu.make_async_copy(clip_hbm, clip_ref, load_sem.at[4])
    load_i.start()
    load_u.start()
    load_w.start()
    load_c.start()
    load_p.start()

    barrier = pltpu.get_barrier_semaphore()
    for d in (1, 2, 3):
        pl.semaphore_signal(barrier, inc=1, device_id=z_device(zp(d)), device_id_type=MESH)
        pl.semaphore_signal(barrier, inc=1, device_id=item_peer(d), device_id_type=MESH)
    pl.semaphore_signal(barrier, inc=1, device_id=partner, device_id_type=MESH)
    load_i.wait()
    load_u.wait()
    pl.semaphore_wait(barrier, 7)

    sent = []

    def remote(src, dst, send, recv, device):
        copy = pltpu.make_async_remote_copy(
            src_ref=src, dst_ref=dst, send_sem=send, recv_sem=recv,
            device_id=device, device_id_type=MESH,
        )
        sent.append(copy)
        return copy

    mine_i = i_block(items, z, core)
    mine_u = users.at[pl.ds(u_at(0), ub)]
    relays = [remote(mine_i, mine_i, rl_send.at[0], rl_recv.at[0], partner)]
    relays[0].start()
    z_copies, u_copies = {}, {}
    for d in (1, 2, 3):
        z_copies[d] = remote(mine_i, mine_i, z_send.at[d], z_recv.at[d], z_device(zp(d)))
        z_copies[d].start()
    for d in (1, 2, 3):
        u_copies[d] = remote(mine_u, mine_u, u_send.at[d], u_recv.at[d], item_peer(d))
        u_copies[d].start()

    def relay(d):
        z_copies[d].wait_recv()
        block = i_block(items, zp(d), core)
        relays.append(remote(block, block, rl_send.at[d], rl_recv.at[d], partner))
        relays[-1].start()

    def i_rows(d, of_core):
        return pl.ds(pl.multiple_of((2 * zp(d) + of_core) * ib, ib), ib)

    own, other = core, 1 - core

    def take_items(d, of_core):
        at = i_rows(d, of_core)
        high, low = split(items[at, :])
        icat[at, 0:width] = high
        icat[at, width : 2 * width] = low
        icat[at, 2 * width : 3 * width] = high

    def take_users(d):
        at = pl.ds(u_at(d), ub)
        high, low = split(users[at, :])
        ucat[at, 0:width] = high
        ucat[at, width : 2 * width] = high
        ucat[at, 2 * width : 3 * width] = low

    scored = set()

    def score(d, *blocks):
        at = pl.ds(u_at(d), ub)
        both = jnp.concatenate([icat[i_rows(*block), :] for block in blocks], axis=0)
        predicted = lax.dot_general(
            ucat[at, :], both, (((1,), (1,)), ((), ())), preferred_element_type=F32
        )
        total = sq_part[at, :] if d in scored else jnp.zeros((ub, lane), F32)
        scored.add(d)
        for n, block in enumerate(blocks):
            col = i_rows(*block)
            weighted = conf[at, col] * (predicted[:, n * ib : (n + 1) * ib] - target[at, col])
            high, low = split(weighted)
            w_high[at, col] = high
            w_low[at, col] = low
            total = total + weighted * weighted
        sq_part[at, :] = total

    load_w.wait()
    load_c.wait()
    load_p.wait()
    tile = 128

    @pl.loop(0, rows // tile)
    def _(t):
        at = pl.ds(pl.multiple_of(t * tile, tile), tile)
        level = prefs[at, :]
        conf[at, :] = 2.0 + (2.0 * weight_ref[...]) * level.astype(F32)
        target[at, :] = jnp.where(level > 0, 1.0, 0.0).astype(F32)

    take_users(0)
    take_items(0, own)
    relay(1)
    take_items(1, own)
    relays[0].wait_recv()
    relays[1].wait_recv()
    take_items(0, other)
    take_items(1, other)
    near = ((0, own), (0, other), (1, own), (1, other))
    far_own, far_other = ((2, own), (3, own)), ((2, other), (3, other))
    score(0, *near)
    for d in (1, 2):
        u_copies[d].wait_recv()
        take_users(d)
        score(d, *near)
    relay(2)
    relay(3)
    take_items(2, own)
    take_items(3, own)
    for d in (0, 1, 2):
        score(d, *far_own)
    relays[2].wait_recv()
    relays[3].wait_recv()
    take_items(2, other)
    take_items(3, other)
    for d in (0, 1, 2):
        score(d, *far_other)
    u_copies[3].wait_recv()
    take_users(3)
    score(3, *near)
    score(3, *far_own)
    score(3, *far_other)
    sq[0] = jnp.sum(sq_part[...].T, axis=0, keepdims=True)

    sq_copies = []
    for d in (3, 1, 2):
        sq_copies.append(remote(sq.at[0], sq.at[d], sq_send.at[d], sq_recv.at[d], item_peer(d)))
        sq_copies[-1].start()

    g_copies = []

    def user_grads(*relations):
        for d in relations:
            at = pl.ds(u_at(d), ub)
            both = mm(w_high[at, :], icat[:, 0 : 2 * width])
            cross = mm(w_low[at, :], icat[:, 0:width])
            grad[at, :] = both[:, 0:width] + (both[:, width:] + cross)
        for d in relations:
            if d > 0:
                at = pl.ds(u_at(d), ub)
                copy = remote(
                    grad.at[at], grad_in.at[d - 1], gr_send.at[d], gr_recv.at[d], item_peer(d)
                )
                g_copies.append(copy)
                copy.start()

    for d in (3, 1, 2, 0):
        user_grads(d)

    users_t[...] = users[...].T
    flat = users_t[...]
    user_sq = jnp.sum(flat * flat, axis=0, keepdims=True)
    for copy in sq_copies:
        copy.wait_recv()
    total_sq = sq[0]
    for d in (1, 2, 3):
        total_sq = total_sq + sq[d]
    bound_scale = 0.001 * jnp.sqrt(jnp.full((1, 1), float(cols * ni * width), F32))
    factor = jnp.minimum(
        1.0, clip_ref[...].astype(F32) * bound_scale / jnp.sqrt(total_sq * user_sq + 1e-06)
    )
    s_high, s_low = split(flat * factor)
    scat[0:width, :] = s_high
    scat[width:, :] = s_low

    pair_copies = {}

    def f_copy(k, c, src_z, to_z, slot):
        piece = pl.ds(c * iq, iq)
        return remote(
            pair_sum.at[src_z, piece], far_in.at[slot, piece],
            fr_send.at[k, c], fr_recv.at[slot, c], z_device(to_z),
        )

    def f_wait(slot, c):
        piece = far_in.at[slot, pl.ds(c * iq, iq)]
        pltpu.make_async_copy(piece, piece, fr_recv.at[slot, c]).wait()

    f_third = [f_copy(3, c, zp(3), zp(3), 3) for c in (0, 1)]

    def forward(d):
        to_z = zp(d)
        pair_copies[d].wait_recv()
        pair_sum[to_z] = i_block(part, to_z, core)[...] + pair_in[to_z]
        if d == 2:
            for c in (0, 1):
                f_copy(2, c, to_z, by_role(zp(1), zp(2)), 2).start()
        if d == 1:
            for c in (0, 1):
                f_copy(1, c, to_z, to_z, 1).start()
        if d == 3:

            @pl.when(inner == 0)
            def _():
                for c in (0, 1):
                    f_third[c].start()

    def item_grads(pair):
        for d in pair:
            col = pl.ds(pl.multiple_of(zp(d) * big, big), big)
            both = mm(scat[...], w_high[:, col])
            cross = mm(scat[0:width, :], w_low[:, col])
            part[col, :] = (both[0:width] + (both[width:] + cross)).T
        for d in pair:
            to_z = zp(d)
            pair_copies[d] = remote(
                i_block(part, to_z, 1 - core), pair_in.at[to_z],
                pr_send.at[d], pr_recv.at[d], partner,
            )
            pair_copies[d].start()

    item_grads((2, 3, 1, 0))
    for d in (2, 3, 1, 0):
        forward(d)

    @pl.when(inner == 1)
    def _():
        to_z = zp(3)
        for c in (0, 1):
            f_wait(2, c)
            piece = pl.ds(c * iq, iq)
            pair_sum[to_z, piece, :] = pair_sum[to_z, piece, :] + far_in[2, piece, :]
            f_third[c].start()

    for copy in g_copies:
        copy.wait_recv()
    user_grad = grad[pl.ds(u_at(0), ub), :]
    for d in (1, 2, 3):
        user_grad = user_grad + grad_in[d - 1]
    user_grad_ref[...] = user_grad

    for c in (0, 1):
        f_wait(1, c)
    item_sum_ref[...] = pair_sum[z] + far_in[1]

    @pl.when(inner == 0)
    def _():
        for c in (0, 1):
            f_wait(2, c)
        item_sum_ref[...] = item_sum_ref[...] + far_in[2]

    for copy in sent:
        copy.wait_send()
    for c in (0, 1):
        f_wait(3, c)
    item_sum_ref[...] = item_sum_ref[...] + far_in[3]


def step_kernel(
    nu, ni,
    prefs_hbm, weight_hbm, clip_hbm, user_hbm, item_hbm,
    user_grad_ref, item_sum_ref,
    prefs, weight_ref, clip_ref, users, items, conf, target, ucat, icat, users_t, w_high, w_low,
    sq, sq_part, grad, grad_in, part, pair_in, pair_sum, far_in, scat,
    load_sem, ug_send, ug_recv, ig_send, ig_recv, rl_send, rl_recv,
    sq_send, sq_recv, gr_send, gr_recv, pr_send, pr_recv, fr_send, fr_recv,
):
    me_u, me_i = lax.axis_index("users"), lax.axis_index("items")
    half = nu // 2
    z, core = me_u // 2, me_u % 2
    partner = (2 * z + 1 - core, me_i)
    rows, cols = prefs.shape
    width = users.shape[1]
    ub, ib = rows // ni, cols // nu

    def u_slot(owner):
        return users.at[pl.ds(pl.multiple_of(owner * ub, ub), ub)]

    def i_slot(ref, owner):
        return ref.at[pl.ds(pl.multiple_of(owner * ib, ib), ib)]

    def item_peer(d):
        return (me_u, paired(me_i, d))

    def z_peer(d):
        return (2 * paired(z, d) + core, me_i)

    load_i = pltpu.make_async_copy(item_hbm, i_slot(items, me_u), load_sem.at[0])
    load_u = pltpu.make_async_copy(user_hbm, u_slot(me_i), load_sem.at[1])
    load_p = pltpu.make_async_copy(prefs_hbm, prefs, load_sem.at[2])
    load_w = pltpu.make_async_copy(weight_hbm, weight_ref, load_sem.at[3])
    load_c = pltpu.make_async_copy(clip_hbm, clip_ref, load_sem.at[4])
    load_i.start()
    load_u.start()
    load_w.start()
    load_c.start()
    load_p.start()

    barrier = pltpu.get_barrier_semaphore()
    for d in range(1, half):
        pl.semaphore_signal(barrier, inc=1, device_id=z_peer(d), device_id_type=MESH)
    for d in range(1, ni):
        pl.semaphore_signal(barrier, inc=1, device_id=item_peer(d), device_id_type=MESH)
    pl.semaphore_signal(barrier, inc=1, device_id=partner, device_id_type=MESH)
    load_i.wait()
    load_u.wait()
    pl.semaphore_wait(barrier, half + ni - 1)

    def remote(src, dst, send, recv, device):
        return pltpu.make_async_remote_copy(
            src_ref=src, dst_ref=dst, send_sem=send, recv_sem=recv,
            device_id=device, device_id_type=MESH,
        )

    mine_i = i_slot(items, me_u)
    mine_u = u_slot(me_i)
    z_copies, relays, u_copies = [], [], []
    relays.append(remote(mine_i, mine_i, rl_send.at[0], rl_recv.at[0], partner))
    relays[0].start()
    for d in range(1, half):
        z_copies.append(remote(mine_i, mine_i, ig_send.at[d], ig_recv.at[d], z_peer(d)))
        z_copies[-1].start()
    for d in range(1, ni):
        u_copies.append(remote(mine_u, mine_u, ug_send.at[d], ug_recv.at[d], item_peer(d)))
        u_copies[-1].start()

    load_w.wait()
    load_c.wait()
    load_p.wait()
    tile = min(rows, 128)

    @pl.loop(0, rows // tile)
    def _(t):
        at = pl.ds(pl.multiple_of(t * tile, tile), tile)
        level = prefs[at, :]
        conf[at, :] = 2.0 + (2.0 * weight_ref[...]) * level.astype(F32)
        target[at, :] = jnp.where(level > 0, 1.0, 0.0).astype(F32)

    big, lane = 256, 128

    def relay(d):
        z_copies[d - 1].wait_recv()
        block = i_slot(items, 2 * paired(z, d) + core)
        relays.append(remote(block, block, rl_send.at[d], rl_recv.at[d], partner))
        relays[-1].start()

    def take_items(start, size):
        at = pl.ds(start, size)
        high, low = split(items[at, :])
        icat[at, 0:width] = high
        icat[at, width : 2 * width] = low
        icat[at, 2 * width : 3 * width] = high

    def take_users(start, size):
        at = pl.ds(start, size)
        high, low = split(users[at, :])
        ucat[at, 0:width] = high
        ucat[at, width : 2 * width] = high
        ucat[at, 2 * width : 3 * width] = low

    def score(row, height, start, extent, first):
        at = pl.ds(row, height)
        left = ucat[at, :]
        total = jnp.zeros((height, lane), F32) if first else sq_part[at, :]
        for k in range(extent // big):
            col = pl.ds(start + k * big, big)
            predicted = lax.dot_general(
                left, icat[col, :], (((1,), (1,)), ((), ())), preferred_element_type=F32
            )
            weighted = conf[at, col] * (predicted - target[at, col])
            high, low = split(weighted)
            w_high[at, col] = high
            w_low[at, col] = low
            square = weighted * weighted
            for m in range(big // lane):
                total = total + square[:, m * lane : (m + 1) * lane]
        sq_part[at, :] = total

    if half == 4 and ni == 4 and ub == big and cols == 4 * big:
        near = pl.multiple_of(z // 2 * (2 * big), 2 * big)

        def i_at(d):
            return pl.multiple_of(paired(z, d) * big, big)

        def u_at(d):
            return pl.multiple_of(paired(me_i, d) * ub, ub)

        relay(1)
        take_users(u_at(0), ub)
        relays[0].wait_recv()
        relays[1].wait_recv()
        take_items(near, 2 * big)
        score(u_at(0), ub, near, 2 * big, True)
        for d in (1, 2):
            u_copies[d - 1].wait_recv()
            take_users(u_at(d), ub)
            score(u_at(d), ub, near, 2 * big, True)
        relay(2)
        relay(3)
        u_copies[2].wait_recv()
        take_users(u_at(3), ub)
        score(u_at(3), ub, near, 2 * big, True)
        for d in (2, 3):
            relays[d].wait_recv()
            take_items(i_at(d), big)
            for t in range(ni):
                score(t * big, big, i_at(d), big, False)
        sq[0] = jnp.sum(sq_part[...].T, axis=0, keepdims=True)
    else:
        for d in range(1, half):
            relay(d)
        for copy in u_copies + relays:
            copy.wait_recv()
        take_items(0, cols)
        take_users(0, rows)

        @pl.loop(0, rows // big)
        def _(t):
            score(pl.multiple_of(t * big, big), big, 0, cols, True)

        sq[0] = jnp.sum(sq_part[...].T, axis=0, keepdims=True)

    sq_copies = []
    for d in range(1, ni):
        sq_copies.append(remote(sq.at[0], sq.at[d], sq_send.at[d], sq_recv.at[d], item_peer(d)))
        sq_copies[-1].start()

    g_copies = []
    for d in list(range(1, ni)) + [0]:
        owner = paired(me_i, d)
        at = pl.ds(pl.multiple_of(owner * ub, ub), ub)
        both = mm(w_high[at, :], icat[:, 0 : 2 * width])
        cross = mm(w_low[at, :], icat[:, 0:width])
        grad[at, :] = both[:, 0:width] + (both[:, width:] + cross)
        if d > 0:
            g_copies.append(
                remote(grad.at[at], grad_in.at[d - 1], gr_send.at[d], gr_recv.at[d], item_peer(d))
            )
            g_copies[-1].start()

    users_t[...] = users[...].T
    flat = users_t[...]
    user_sq = jnp.sum(flat * flat, axis=0, keepdims=True)
    for copy in sq_copies:
        copy.wait_recv()
    total_sq = sq[0]
    for d in range(1, ni):
        total_sq = total_sq + sq[d]
    bound_scale = 0.001 * jnp.sqrt(jnp.full((1, 1), float(cols * ni * width), F32))
    factor = jnp.minimum(
        1.0, clip_ref[...].astype(F32) * bound_scale / jnp.sqrt(total_sq * user_sq + 1e-06)
    )
    s_high, s_low = split(flat * factor)
    scat[0:width, :] = s_high
    scat[width:, :] = s_low

    chunk = max(2 * ib, min(256, cols))
    groups = cols // chunk
    per = half // groups
    my_group = z // per
    pair_copies, far_copies = {}, {}

    def relations(order):
        return [(groups - order) * per + e for e in range(per)]

    def forward(order):
        for d in relations(order):
            to_z = paired(z, d)
            pair_copies[d].wait_recv()
            pair_sum[to_z] = i_slot(part, 2 * to_z + core)[...] + pair_in[to_z]
            if d > 0:
                far_copies[d] = remote(
                    pair_sum.at[to_z], far_in.at[d], fr_send.at[d], fr_recv.at[d], z_peer(d)
                )
                far_copies[d].start()

    for order in range(1, groups + 1):
        group = paired(my_group, groups - order)
        col = pl.ds(pl.multiple_of(group * chunk, chunk), chunk)
        both = mm(scat[...], w_high[:, col])
        cross = mm(scat[0:width, :], w_low[:, col])
        part[col, :] = (both[0:width] + (both[width:] + cross)).T
        for d in relations(order):
            to_z = paired(z, d)
            pair_copies[d] = remote(
                i_slot(part, 2 * to_z + 1 - core), pair_in.at[to_z],
                pr_send.at[d], pr_recv.at[d], partner,
            )
            pair_copies[d].start()
        if order > 1:
            forward(order - 1)
    forward(groups)

    for copy in g_copies:
        copy.wait_recv()
    user_grad = grad[pl.ds(pl.multiple_of(me_i * ub, ub), ub), :]
    for d in range(1, ni):
        user_grad = user_grad + grad_in[d - 1]
    user_grad_ref[...] = user_grad

    sent = z_copies + relays + u_copies + sq_copies + g_copies + list(pair_copies.values())
    for copy in sent + list(far_copies.values()):
        copy.wait_send()
    item_sum = pair_sum[z]
    for d in range(1, half):
        far_copies[d].wait_recv()
        item_sum = item_sum + far_in[d]
    item_sum_ref[...] = item_sum


def update_kernel(
    user_grad, item_sum, user_emb, user_acc, item_emb, item_acc, noise,
    new_user_emb, new_user_acc, new_item_emb, new_item_acc,
):
    grad = user_grad[...]
    acc = user_acc[...] + grad * grad
    new_user_acc[...] = acc
    new_user_emb[...] = user_emb[...] - learn_rate * grad / jnp.sqrt(acc)
    grad = item_sum[...] + noise_step * noise[...].astype(F32)
    acc = item_acc[...] + grad * grad
    new_item_acc[...] = acc
    new_item_emb[...] = item_emb[...] - learn_rate * grad / jnp.sqrt(acc)


def local(prefs, item_weight, clip_units, user_emb, user_acc, item_emb, item_acc, noise):
    nu, ni = lax.axis_size("users"), lax.axis_size("items")
    rows, cols = prefs.shape
    ub, width = user_emb.shape
    ib = item_emb.shape[0]
    half = nu // 2
    vmem = pl.BlockSpec(memory_space=pltpu.VMEM)
    hbm = pl.BlockSpec(memory_space=pltpu.HBM)
    dma = pltpu.SemaphoreType.DMA
    line = nu == 8 and ni == 4 and ub == 256 and ib == 128 and width == 128
    if line:
        kernel = line_kernel
        semaphores = [
            dma((5,)),
            dma((4,)), dma((4,)),
            dma((4,)), dma((4,)),
            dma((4,)), dma((4,)),
            dma((4,)), dma((4,)),
            dma((4,)), dma((4,)),
            dma((4,)), dma((4,)),
            dma((4, 2)), dma((4, 2)),
        ]
    else:
        kernel = functools.partial(step_kernel, nu, ni)
        semaphores = [
            dma((5,)),
            dma((ni,)), dma((ni,)),
            dma((half,)), dma((half,)),
            dma((half,)), dma((half,)),
            dma((ni,)), dma((ni,)),
            dma((ni + 1,)), dma((ni + 1,)),
            dma((half,)), dma((half,)),
            dma((half,)), dma((half,)),
        ]
    user_grad, item_sum = pl.pallas_call(
        kernel,
        out_shape=(
            jax.ShapeDtypeStruct((ub, width), F32),
            jax.ShapeDtypeStruct((ib, width), F32),
        ),
        in_specs=[hbm] * 5,
        out_specs=(vmem, vmem),
        scratch_shapes=[
            pltpu.VMEM((rows, cols), jnp.int32),
            pltpu.VMEM((1, cols), F32),
            pltpu.VMEM((1, rows), jnp.int32),
            pltpu.VMEM((rows, width), F32),
            pltpu.VMEM((cols, width), F32),
            pltpu.VMEM((rows, cols), F32),
            pltpu.VMEM((rows, cols), F32),
            pltpu.VMEM((rows, 3 * width), BF16),
            pltpu.VMEM((cols, 3 * width), BF16),
            pltpu.VMEM((width, rows), F32),
            pltpu.VMEM((rows, cols), BF16),
            pltpu.VMEM((rows, cols), BF16),
            pltpu.VMEM((ni, 1, rows), F32),
            pltpu.VMEM((rows, 128), F32),
            pltpu.VMEM((rows, width), F32),
            pltpu.VMEM((ni - 1, ub, width), F32),
            pltpu.VMEM((cols, width), F32),
            pltpu.VMEM((half, ib, width), F32),
            pltpu.VMEM((half, ib, width), F32),
            pltpu.VMEM((half, ib, width), F32),
            pltpu.VMEM((2 * width, rows), BF16),
        ] + semaphores,
        compiler_params=pltpu.CompilerParams(
            collective_id=0, has_side_effects=True, vmem_limit_bytes=48 * 1024 * 1024
        ),
    )(*[pltpu.with_memory_space_constraint(x, pltpu.HBM) for x in (prefs, item_weight[None, :], clip_units[None, :], user_emb, item_emb)])
    user_shape = jax.ShapeDtypeStruct((ub, width), F32)
    item_shape = jax.ShapeDtypeStruct((ib, width), F32)
    vmem = pl.BlockSpec(memory_space=pltpu.VMEM)
    return pl.pallas_call(
        update_kernel,
        out_shape=(user_shape, user_shape, item_shape, item_shape),
        in_specs=[vmem] * 7,
        out_specs=(vmem,) * 4,
        compiler_params=pltpu.CompilerParams(vmem_limit_bytes=4 * 1024 * 1024),
    )(user_grad, item_sum, user_emb, user_acc, item_emb, item_acc, noise)


def solution(mesh):
    placed = (
        P("users", "items"),
        P("items"),
        P("users"),
        P(("users", "items"), None),
        P(("users", "items"), None),
        P(("items", "users"), None),
        P(("items", "users"), None),
        P(("items", "users"), None),
    )
    return jax.shard_map(
        local,
        mesh=mesh,
        in_specs=placed,
        out_specs=(
            P(("users", "items"), None),
            P(("users", "items"), None),
            P(("items", "users"), None),
            P(("items", "users"), None),
        ),
        check_vma=False,
    )
```

```python
import functools

import jax
import jax.numpy as jnp
from jax import lax
from jax.experimental import pallas as pl
from jax.experimental.pallas import tpu as pltpu
from jax.sharding import PartitionSpec as P

noise_step = 0.05
learn_rate = 0.5
MESH = pl.DeviceIdType.MESH
F32 = jnp.float32
BF16 = jnp.bfloat16


def split(x):
    high = x.astype(BF16)
    return high, (x - high.astype(F32)).astype(BF16)


def mm(a, b):
    return jnp.dot(a, b, preferred_element_type=F32)


def paired(here, relation):
    bit = 1
    while bit <= relation:
        if relation & bit:
            here = here + bit - 2 * bit * (here // bit % 2)
        bit *= 2
    return here


def line_kernel(
    prefs_hbm, weight_hbm, clip_hbm, user_hbm, item_hbm,
    user_grad_ref, item_sum_ref,
    prefs, weight_ref, clip_ref, users, items, conf, target, ucat, icat, users_t, w_high, w_low,
    sq, sq_part, grad, grad_in, part, pair_in, pair_sum, far_in, scat,
    load_sem, u_send, u_recv, z_send, z_recv, rl_send, rl_recv,
    sq_send, sq_recv, gr_send, gr_recv, pr_send, pr_recv, fr_send, fr_recv,
):
    ni, half = 4, 4
    me_u, me_i = lax.axis_index("users"), lax.axis_index("items")
    z, core = me_u // 2, me_u % 2
    inner = (z + 1) // 2 % 2
    partner = (2 * z + 1 - core, me_i)
    rows, cols = prefs.shape
    width = users.shape[1]
    ub, ib = rows // ni, cols // (2 * half)
    big, lane = 2 * ib, 128
    iq = ib // 2

    def zp(d):
        return paired(z, d)

    def by_role(at_end, between):
        return at_end + inner * (between - at_end)

    def u_at(d):
        return pl.multiple_of(paired(me_i, d) * ub, ub)

    def i_block(ref, to_z, of_core):
        return ref.at[pl.ds(pl.multiple_of((2 * to_z + of_core) * ib, ib), ib)]

    def item_peer(d):
        return (me_u, paired(me_i, d))

    def z_device(to_z):
        return (2 * to_z + core, me_i)

    load_i = pltpu.make_async_copy(item_hbm, i_block(items, z, core), load_sem.at[0])
    load_u = pltpu.make_async_copy(user_hbm, users.at[pl.ds(u_at(0), ub)], load_sem.at[1])
    load_p = pltpu.make_async_copy(prefs_hbm, prefs, load_sem.at[2])
    load_w = pltpu.make_async_copy(weight_hbm, weight_ref, load_sem.at[3])
    load_c = pltpu.make_async_copy(clip_hbm, clip_ref, load_sem.at[4])
    barrier = pltpu.get_barrier_semaphore()
    for d in (1, 2, 3):
        pl.semaphore_signal(barrier, inc=1, device_id=z_device(zp(d)), device_id_type=MESH)
        pl.semaphore_signal(barrier, inc=1, device_id=item_peer(d), device_id_type=MESH)
    pl.semaphore_signal(barrier, inc=1, device_id=partner, device_id_type=MESH)
    load_i.start()
    load_u.start()
    load_w.start()
    load_c.start()
    load_p.start()
    load_i.wait()
    load_u.wait()
    pl.semaphore_wait(barrier, 7)

    sent = []

    def remote(src, dst, send, recv, device):
        copy = pltpu.make_async_remote_copy(
            src_ref=src, dst_ref=dst, send_sem=send, recv_sem=recv,
            device_id=device, device_id_type=MESH,
        )
        sent.append(copy)
        return copy

    mine_i = i_block(items, z, core)
    mine_u = users.at[pl.ds(u_at(0), ub)]
    relays = [remote(mine_i, mine_i, rl_send.at[0], rl_recv.at[0], partner)]
    relays[0].start()
    z_copies, u_copies = {}, {}
    for d in (1, 2, 3):
        z_copies[d] = remote(mine_i, mine_i, z_send.at[d], z_recv.at[d], z_device(zp(d)))
        z_copies[d].start()
    for d in (1, 3, 2):
        u_copies[d] = remote(mine_u, mine_u, u_send.at[d], u_recv.at[d], item_peer(d))
        u_copies[d].start()

    def relay(d):
        z_copies[d].wait_recv()
        block = i_block(items, zp(d), core)
        relays.append(remote(block, block, rl_send.at[d], rl_recv.at[d], partner))
        relays[-1].start()

    def i_rows(d, of_core):
        return pl.ds(pl.multiple_of((2 * zp(d) + of_core) * ib, ib), ib)

    own, other = core, 1 - core

    def take_items(d, of_core):
        at = i_rows(d, of_core)
        high, low = split(items[at, :])
        icat[at, 0:width] = high
        icat[at, width : 2 * width] = low
        icat[at, 2 * width : 3 * width] = high

    def take_users(d):
        at = pl.ds(u_at(d), ub)
        high, low = split(users[at, :])
        ucat[at, 0:width] = high
        ucat[at, width : 2 * width] = high
        ucat[at, 2 * width : 3 * width] = low

    def sum_squares(d):
        at = pl.ds(u_at(d), ub)
        sq[0, :, at] = jnp.sum(sq_part[at, :].T, axis=0, keepdims=True)

    scored = set()

    def score(d, *blocks):
        at = pl.ds(u_at(d), ub)
        both = jnp.concatenate([icat[i_rows(*block), :] for block in blocks], axis=0)
        predicted = lax.dot_general(
            ucat[at, :], both, (((1,), (1,)), ((), ())), preferred_element_type=F32
        )
        total = sq_part[at, :] if d in scored else jnp.zeros((ub, lane), F32)
        scored.add(d)
        for n, block in enumerate(blocks):
            col = i_rows(*block)
            weighted = conf[at, col] * (predicted[:, n * ib : (n + 1) * ib] - target[at, col])
            high, low = split(weighted)
            w_high[at, col] = high
            w_low[at, col] = low
            total = total + weighted * weighted
        sq_part[at, :] = total

    load_w.wait()
    load_c.wait()
    load_p.wait()
    tile = 128

    @pl.loop(0, rows // tile)
    def _(t):
        at = pl.ds(pl.multiple_of(t * tile, tile), tile)
        level = prefs[at, :]
        conf[at, :] = 2.0 + (2.0 * weight_ref[...]) * level.astype(F32)
        target[at, :] = jnp.where(level > 0, 1.0, 0.0).astype(F32)

    take_users(0)
    take_items(0, own)
    relay(1)
    take_items(1, own)
    relays[0].wait_recv()
    relays[1].wait_recv()
    take_items(0, other)
    take_items(1, other)
    near = ((0, own), (0, other), (1, own), (1, other))
    far_own, far_other = ((2, own), (3, own)), ((2, other), (3, other))
    score(0, *near)
    for d in (1, 2):
        u_copies[d].wait_recv()
        take_users(d)
        score(d, *near)
    relay(2)
    relay(3)
    take_items(2, own)
    take_items(3, own)
    for d in (0, 1, 2):
        score(d, *far_own)
    relays[2].wait_recv()
    relays[3].wait_recv()
    take_items(2, other)
    take_items(3, other)
    for d in (0, 1, 2):
        score(d, *far_other)
    for d in (0, 1, 2):
        sum_squares(d)
    u_copies[3].wait_recv()
    take_users(3)
    score(3, *near)
    score(3, *far_own)
    score(3, *far_other)
    sum_squares(3)

    sq_copies = []
    for d in (3, 1, 2):
        sq_copies.append(remote(sq.at[0], sq.at[d], sq_send.at[d], sq_recv.at[d], item_peer(d)))
        sq_copies[-1].start()

    g_copies = []

    def user_grads(*relations):
        for d in relations:
            at = pl.ds(u_at(d), ub)
            both = mm(w_high[at, :], icat[:, 0 : 2 * width])
            cross = mm(w_low[at, :], icat[:, 0:width])
            grad[at, :] = both[:, 0:width] + (both[:, width:] + cross)
        for d in relations:
            if d > 0:
                at = pl.ds(u_at(d), ub)
                copy = remote(
                    grad.at[at], grad_in.at[d - 1], gr_send.at[d], gr_recv.at[d], item_peer(d)
                )
                g_copies.append(copy)
                copy.start()

    for d in (3, 1, 2):
        user_grads(d)

    users_t[...] = users[...].T
    flat = users_t[...]
    user_sq = jnp.sum(flat * flat, axis=0, keepdims=True)
    for copy in sq_copies:
        copy.wait_recv()
    total_sq = sq[0]
    for d in (1, 2, 3):
        total_sq = total_sq + sq[d]
    bound_scale = 0.001 * jnp.sqrt(jnp.full((1, 1), float(cols * ni * width), F32))
    factor = jnp.minimum(
        1.0, clip_ref[...].astype(F32) * bound_scale / jnp.sqrt(total_sq * user_sq + 1e-06)
    )
    s_high, s_low = split(flat * factor)
    scat[0:width, :] = s_high
    scat[width:, :] = s_low

    pair_copies = {}

    def f_copy(k, c, src_z, to_z, slot):
        piece = pl.ds(c * iq, iq)
        return remote(
            pair_sum.at[src_z, piece], far_in.at[slot, piece],
            fr_send.at[k, c], fr_recv.at[slot, c], z_device(to_z),
        )

    def f_wait(slot, c):
        piece = far_in.at[slot, pl.ds(c * iq, iq)]
        pltpu.make_async_copy(piece, piece, fr_recv.at[slot, c]).wait()

    f_third = [f_copy(3, c, zp(3), zp(3), 3) for c in (0, 1)]

    def forward(d):
        to_z = zp(d)
        pair_copies[d].wait_recv()
        pair_sum[to_z] = i_block(part, to_z, core)[...] + pair_in[to_z]
        if d == 2:
            for c in (0, 1):
                f_copy(2, c, to_z, by_role(zp(1), zp(2)), 2).start()
        if d == 1:
            for c in (0, 1):
                f_copy(1, c, to_z, to_z, 1).start()
        if d == 3:

            @pl.when(inner == 0)
            def _():
                for c in (0, 1):
                    f_third[c].start()

    def item_grads(pair):
        for d in pair:
            col = pl.ds(pl.multiple_of(zp(d) * big, big), big)
            both = mm(scat[...], w_high[:, col])
            cross = mm(scat[0:width, :], w_low[:, col])
            part[col, :] = (both[0:width] + (both[width:] + cross)).T
        for d in pair:
            to_z = zp(d)
            pair_copies[d] = remote(
                i_block(part, to_z, 1 - core), pair_in.at[to_z],
                pr_send.at[d], pr_recv.at[d], partner,
            )
            pair_copies[d].start()

    item_grads((2, 3, 1, 0))
    for d in (2, 3, 1, 0):
        forward(d)
    user_grads(0)

    @pl.when(inner == 1)
    def _():
        to_z = zp(3)
        for c in (0, 1):
            f_wait(2, c)
            piece = pl.ds(c * iq, iq)
            pair_sum[to_z, piece, :] = pair_sum[to_z, piece, :] + far_in[2, piece, :]
            f_third[c].start()

    for copy in g_copies:
        copy.wait_recv()
    user_grad = grad[pl.ds(u_at(0), ub), :]
    for d in (1, 2, 3):
        user_grad = user_grad + grad_in[d - 1]
    user_grad_ref[...] = user_grad

    for c in (0, 1):
        f_wait(1, c)
    item_sum_ref[...] = pair_sum[z] + far_in[1]

    @pl.when(inner == 0)
    def _():
        for c in (0, 1):
            f_wait(2, c)
        item_sum_ref[...] = item_sum_ref[...] + far_in[2]

    for copy in sent:
        copy.wait_send()
    for c in (0, 1):
        f_wait(3, c)
    item_sum_ref[...] = item_sum_ref[...] + far_in[3]


def step_kernel(
    nu, ni,
    prefs_hbm, weight_hbm, clip_hbm, user_hbm, item_hbm,
    user_grad_ref, item_sum_ref,
    prefs, weight_ref, clip_ref, users, items, conf, target, ucat, icat, users_t, w_high, w_low,
    sq, sq_part, grad, grad_in, part, pair_in, pair_sum, far_in, scat,
    load_sem, ug_send, ug_recv, ig_send, ig_recv, rl_send, rl_recv,
    sq_send, sq_recv, gr_send, gr_recv, pr_send, pr_recv, fr_send, fr_recv,
):
    me_u, me_i = lax.axis_index("users"), lax.axis_index("items")
    half = nu // 2
    z, core = me_u // 2, me_u % 2
    partner = (2 * z + 1 - core, me_i)
    rows, cols = prefs.shape
    width = users.shape[1]
    ub, ib = rows // ni, cols // nu

    def u_slot(owner):
        return users.at[pl.ds(pl.multiple_of(owner * ub, ub), ub)]

    def i_slot(ref, owner):
        return ref.at[pl.ds(pl.multiple_of(owner * ib, ib), ib)]

    def item_peer(d):
        return (me_u, paired(me_i, d))

    def z_peer(d):
        return (2 * paired(z, d) + core, me_i)

    load_i = pltpu.make_async_copy(item_hbm, i_slot(items, me_u), load_sem.at[0])
    load_u = pltpu.make_async_copy(user_hbm, u_slot(me_i), load_sem.at[1])
    load_p = pltpu.make_async_copy(prefs_hbm, prefs, load_sem.at[2])
    load_w = pltpu.make_async_copy(weight_hbm, weight_ref, load_sem.at[3])
    load_c = pltpu.make_async_copy(clip_hbm, clip_ref, load_sem.at[4])
    load_i.start()
    load_u.start()
    load_w.start()
    load_c.start()
    load_p.start()

    barrier = pltpu.get_barrier_semaphore()
    for d in range(1, half):
        pl.semaphore_signal(barrier, inc=1, device_id=z_peer(d), device_id_type=MESH)
    for d in range(1, ni):
        pl.semaphore_signal(barrier, inc=1, device_id=item_peer(d), device_id_type=MESH)
    pl.semaphore_signal(barrier, inc=1, device_id=partner, device_id_type=MESH)
    load_i.wait()
    load_u.wait()
    pl.semaphore_wait(barrier, half + ni - 1)

    def remote(src, dst, send, recv, device):
        return pltpu.make_async_remote_copy(
            src_ref=src, dst_ref=dst, send_sem=send, recv_sem=recv,
            device_id=device, device_id_type=MESH,
        )

    mine_i = i_slot(items, me_u)
    mine_u = u_slot(me_i)
    z_copies, relays, u_copies = [], [], []
    relays.append(remote(mine_i, mine_i, rl_send.at[0], rl_recv.at[0], partner))
    relays[0].start()
    for d in range(1, half):
        z_copies.append(remote(mine_i, mine_i, ig_send.at[d], ig_recv.at[d], z_peer(d)))
        z_copies[-1].start()
    for d in range(1, ni):
        u_copies.append(remote(mine_u, mine_u, ug_send.at[d], ug_recv.at[d], item_peer(d)))
        u_copies[-1].start()

    load_w.wait()
    load_c.wait()
    load_p.wait()
    tile = min(rows, 128)

    @pl.loop(0, rows // tile)
    def _(t):
        at = pl.ds(pl.multiple_of(t * tile, tile), tile)
        level = prefs[at, :]
        conf[at, :] = 2.0 + (2.0 * weight_ref[...]) * level.astype(F32)
        target[at, :] = jnp.where(level > 0, 1.0, 0.0).astype(F32)

    big, lane = 256, 128

    def relay(d):
        z_copies[d - 1].wait_recv()
        block = i_slot(items, 2 * paired(z, d) + core)
        relays.append(remote(block, block, rl_send.at[d], rl_recv.at[d], partner))
        relays[-1].start()

    def take_items(start, size):
        at = pl.ds(start, size)
        high, low = split(items[at, :])
        icat[at, 0:width] = high
        icat[at, width : 2 * width] = low
        icat[at, 2 * width : 3 * width] = high

    def take_users(start, size):
        at = pl.ds(start, size)
        high, low = split(users[at, :])
        ucat[at, 0:width] = high
        ucat[at, width : 2 * width] = high
        ucat[at, 2 * width : 3 * width] = low

    def score(row, height, start, extent, first):
        at = pl.ds(row, height)
        left = ucat[at, :]
        total = jnp.zeros((height, lane), F32) if first else sq_part[at, :]
        for k in range(extent // big):
            col = pl.ds(start + k * big, big)
            predicted = lax.dot_general(
                left, icat[col, :], (((1,), (1,)), ((), ())), preferred_element_type=F32
            )
            weighted = conf[at, col] * (predicted - target[at, col])
            high, low = split(weighted)
            w_high[at, col] = high
            w_low[at, col] = low
            square = weighted * weighted
            for m in range(big // lane):
                total = total + square[:, m * lane : (m + 1) * lane]
        sq_part[at, :] = total

    if half == 4 and ni == 4 and ub == big and cols == 4 * big:
        near = pl.multiple_of(z // 2 * (2 * big), 2 * big)

        def i_at(d):
            return pl.multiple_of(paired(z, d) * big, big)

        def u_at(d):
            return pl.multiple_of(paired(me_i, d) * ub, ub)

        relay(1)
        take_users(u_at(0), ub)
        relays[0].wait_recv()
        relays[1].wait_recv()
        take_items(near, 2 * big)
        score(u_at(0), ub, near, 2 * big, True)
        for d in (1, 2):
            u_copies[d - 1].wait_recv()
            take_users(u_at(d), ub)
            score(u_at(d), ub, near, 2 * big, True)
        relay(2)
        relay(3)
        u_copies[2].wait_recv()
        take_users(u_at(3), ub)
        score(u_at(3), ub, near, 2 * big, True)
        for d in (2, 3):
            relays[d].wait_recv()
            take_items(i_at(d), big)
            for t in range(ni):
                score(t * big, big, i_at(d), big, False)
        sq[0] = jnp.sum(sq_part[...].T, axis=0, keepdims=True)
    else:
        for d in range(1, half):
            relay(d)
        for copy in u_copies + relays:
            copy.wait_recv()
        take_items(0, cols)
        take_users(0, rows)

        @pl.loop(0, rows // big)
        def _(t):
            score(pl.multiple_of(t * big, big), big, 0, cols, True)

        sq[0] = jnp.sum(sq_part[...].T, axis=0, keepdims=True)

    sq_copies = []
    for d in range(1, ni):
        sq_copies.append(remote(sq.at[0], sq.at[d], sq_send.at[d], sq_recv.at[d], item_peer(d)))
        sq_copies[-1].start()

    g_copies = []
    for d in list(range(1, ni)) + [0]:
        owner = paired(me_i, d)
        at = pl.ds(pl.multiple_of(owner * ub, ub), ub)
        both = mm(w_high[at, :], icat[:, 0 : 2 * width])
        cross = mm(w_low[at, :], icat[:, 0:width])
        grad[at, :] = both[:, 0:width] + (both[:, width:] + cross)
        if d > 0:
            g_copies.append(
                remote(grad.at[at], grad_in.at[d - 1], gr_send.at[d], gr_recv.at[d], item_peer(d))
            )
            g_copies[-1].start()

    users_t[...] = users[...].T
    flat = users_t[...]
    user_sq = jnp.sum(flat * flat, axis=0, keepdims=True)
    for copy in sq_copies:
        copy.wait_recv()
    total_sq = sq[0]
    for d in range(1, ni):
        total_sq = total_sq + sq[d]
    bound_scale = 0.001 * jnp.sqrt(jnp.full((1, 1), float(cols * ni * width), F32))
    factor = jnp.minimum(
        1.0, clip_ref[...].astype(F32) * bound_scale / jnp.sqrt(total_sq * user_sq + 1e-06)
    )
    s_high, s_low = split(flat * factor)
    scat[0:width, :] = s_high
    scat[width:, :] = s_low

    chunk = max(2 * ib, min(256, cols))
    groups = cols // chunk
    per = half // groups
    my_group = z // per
    pair_copies, far_copies = {}, {}

    def relations(order):
        return [(groups - order) * per + e for e in range(per)]

    def forward(order):
        for d in relations(order):
            to_z = paired(z, d)
            pair_copies[d].wait_recv()
            pair_sum[to_z] = i_slot(part, 2 * to_z + core)[...] + pair_in[to_z]
            if d > 0:
                far_copies[d] = remote(
                    pair_sum.at[to_z], far_in.at[d], fr_send.at[d], fr_recv.at[d], z_peer(d)
                )
                far_copies[d].start()

    for order in range(1, groups + 1):
        group = paired(my_group, groups - order)
        col = pl.ds(pl.multiple_of(group * chunk, chunk), chunk)
        both = mm(scat[...], w_high[:, col])
        cross = mm(scat[0:width, :], w_low[:, col])
        part[col, :] = (both[0:width] + (both[width:] + cross)).T
        for d in relations(order):
            to_z = paired(z, d)
            pair_copies[d] = remote(
                i_slot(part, 2 * to_z + 1 - core), pair_in.at[to_z],
                pr_send.at[d], pr_recv.at[d], partner,
            )
            pair_copies[d].start()
        if order > 1:
            forward(order - 1)
    forward(groups)

    for copy in g_copies:
        copy.wait_recv()
    user_grad = grad[pl.ds(pl.multiple_of(me_i * ub, ub), ub), :]
    for d in range(1, ni):
        user_grad = user_grad + grad_in[d - 1]
    user_grad_ref[...] = user_grad

    sent = z_copies + relays + u_copies + sq_copies + g_copies + list(pair_copies.values())
    for copy in sent + list(far_copies.values()):
        copy.wait_send()
    item_sum = pair_sum[z]
    for d in range(1, half):
        far_copies[d].wait_recv()
        item_sum = item_sum + far_in[d]
    item_sum_ref[...] = item_sum


def update_kernel(
    user_grad, item_sum, user_emb, user_acc, item_emb, item_acc, noise,
    new_user_emb, new_user_acc, new_item_emb, new_item_acc,
):
    grad = user_grad[...]
    acc = user_acc[...] + grad * grad
    new_user_acc[...] = acc
    new_user_emb[...] = user_emb[...] - learn_rate * grad / jnp.sqrt(acc)
    grad = item_sum[...] + noise_step * noise[...].astype(F32)
    acc = item_acc[...] + grad * grad
    new_item_acc[...] = acc
    new_item_emb[...] = item_emb[...] - learn_rate * grad / jnp.sqrt(acc)


def local(prefs, item_weight, clip_units, user_emb, user_acc, item_emb, item_acc, noise):
    nu, ni = lax.axis_size("users"), lax.axis_size("items")
    rows, cols = prefs.shape
    ub, width = user_emb.shape
    ib = item_emb.shape[0]
    half = nu // 2
    vmem = pl.BlockSpec(memory_space=pltpu.VMEM)
    hbm = pl.BlockSpec(memory_space=pltpu.HBM)
    dma = pltpu.SemaphoreType.DMA
    line = nu == 8 and ni == 4 and ub == 256 and ib == 128 and width == 128
    if line:
        kernel = line_kernel
        semaphores = [
            dma((5,)),
            dma((4,)), dma((4,)),
            dma((4,)), dma((4,)),
            dma((4,)), dma((4,)),
            dma((4,)), dma((4,)),
            dma((4,)), dma((4,)),
            dma((4,)), dma((4,)),
            dma((4, 2)), dma((4, 2)),
        ]
    else:
        kernel = functools.partial(step_kernel, nu, ni)
        semaphores = [
            dma((5,)),
            dma((ni,)), dma((ni,)),
            dma((half,)), dma((half,)),
            dma((half,)), dma((half,)),
            dma((ni,)), dma((ni,)),
            dma((ni + 1,)), dma((ni + 1,)),
            dma((half,)), dma((half,)),
            dma((half,)), dma((half,)),
        ]
    user_grad, item_sum = pl.pallas_call(
        kernel,
        out_shape=(
            jax.ShapeDtypeStruct((ub, width), F32),
            jax.ShapeDtypeStruct((ib, width), F32),
        ),
        in_specs=[hbm] * 5,
        out_specs=(vmem, vmem),
        scratch_shapes=[
            pltpu.VMEM((rows, cols), jnp.int32),
            pltpu.VMEM((1, cols), F32),
            pltpu.VMEM((1, rows), jnp.int32),
            pltpu.VMEM((rows, width), F32),
            pltpu.VMEM((cols, width), F32),
            pltpu.VMEM((rows, cols), F32),
            pltpu.VMEM((rows, cols), F32),
            pltpu.VMEM((rows, 3 * width), BF16),
            pltpu.VMEM((cols, 3 * width), BF16),
            pltpu.VMEM((width, rows), F32),
            pltpu.VMEM((rows, cols), BF16),
            pltpu.VMEM((rows, cols), BF16),
            pltpu.VMEM((ni, 1, rows), F32),
            pltpu.VMEM((rows, 128), F32),
            pltpu.VMEM((rows, width), F32),
            pltpu.VMEM((ni - 1, ub, width), F32),
            pltpu.VMEM((cols, width), F32),
            pltpu.VMEM((half, ib, width), F32),
            pltpu.VMEM((half, ib, width), F32),
            pltpu.VMEM((half, ib, width), F32),
            pltpu.VMEM((2 * width, rows), BF16),
        ] + semaphores,
        compiler_params=pltpu.CompilerParams(
            collective_id=0, has_side_effects=True, vmem_limit_bytes=48 * 1024 * 1024
        ),
    )(*[pltpu.with_memory_space_constraint(x, pltpu.HBM) for x in (prefs, item_weight[None, :], clip_units[None, :], user_emb, item_emb)])
    user_shape = jax.ShapeDtypeStruct((ub, width), F32)
    item_shape = jax.ShapeDtypeStruct((ib, width), F32)
    vmem = pl.BlockSpec(memory_space=pltpu.VMEM)
    return pl.pallas_call(
        update_kernel,
        out_shape=(user_shape, user_shape, item_shape, item_shape),
        in_specs=[vmem] * 7,
        out_specs=(vmem,) * 4,
        compiler_params=pltpu.CompilerParams(vmem_limit_bytes=4 * 1024 * 1024),
    )(user_grad, item_sum, user_emb, user_acc, item_emb, item_acc, noise)


def solution(mesh):
    placed = (
        P("users", "items"),
        P("items"),
        P("users"),
        P(("users", "items"), None),
        P(("users", "items"), None),
        P(("items", "users"), None),
        P(("items", "users"), None),
        P(("items", "users"), None),
    )
    return jax.shard_map(
        local,
        mesh=mesh,
        in_specs=placed,
        out_specs=(
            P(("users", "items"), None),
            P(("users", "items"), None),
            P(("items", "users"), None),
            P(("items", "users"), None),
        ),
        check_vma=False,
    )
```

```python
import functools

import jax
import jax.numpy as jnp
from jax import lax
from jax.experimental import pallas as pl
from jax.experimental.pallas import tpu as pltpu
from jax.sharding import PartitionSpec as P

noise_step = 0.05
learn_rate = 0.5
MESH = pl.DeviceIdType.MESH
F32 = jnp.float32
BF16 = jnp.bfloat16


def split(x):
    high = x.astype(BF16)
    return high, (x - high.astype(F32)).astype(BF16)


def mm(a, b):
    return jnp.dot(a, b, preferred_element_type=F32)


def paired(here, relation):
    bit = 1
    while bit <= relation:
        if relation & bit:
            here = here + bit - 2 * bit * (here // bit % 2)
        bit *= 2
    return here


def line_kernel(
    prefs_hbm, weight_hbm, clip_hbm, user_hbm, item_hbm,
    user_grad_ref, item_sum_ref,
    prefs, weight_ref, clip_ref, users, items, conf, target, ucat, icat, users_t, w_high, w_low,
    sq, sq_part, grad, grad_in, part, pair_in, pair_sum, far_in, scat,
    load_sem, u_send, u_recv, z_send, z_recv, rl_send, rl_recv,
    sq_send, sq_recv, gr_send, gr_recv, pr_send, pr_recv, fr_send, fr_recv,
):
    ni, half = 4, 4
    me_u, me_i = lax.axis_index("users"), lax.axis_index("items")
    z, core = me_u // 2, me_u % 2
    inner = (z + 1) // 2 % 2
    partner = (2 * z + 1 - core, me_i)
    rows, cols = prefs.shape
    width = users.shape[1]
    ub, ib = rows // ni, cols // (2 * half)
    big, lane = 2 * ib, 128
    iq = ib // 2

    def zp(d):
        return paired(z, d)

    def by_role(at_end, between):
        return at_end + inner * (between - at_end)

    def u_at(d):
        return pl.multiple_of(paired(me_i, d) * ub, ub)

    def i_block(ref, to_z, of_core):
        return ref.at[pl.ds(pl.multiple_of((2 * to_z + of_core) * ib, ib), ib)]

    def item_peer(d):
        return (me_u, paired(me_i, d))

    def z_device(to_z):
        return (2 * to_z + core, me_i)

    load_i = pltpu.make_async_copy(item_hbm, i_block(items, z, core), load_sem.at[0])
    load_u = pltpu.make_async_copy(user_hbm, users.at[pl.ds(u_at(0), ub)], load_sem.at[1])
    load_p = pltpu.make_async_copy(prefs_hbm, prefs, load_sem.at[2])
    load_w = pltpu.make_async_copy(weight_hbm, weight_ref, load_sem.at[3])
    load_c = pltpu.make_async_copy(clip_hbm, clip_ref, load_sem.at[4])
    barrier = pltpu.get_barrier_semaphore()
    for d in (1, 2, 3):
        pl.semaphore_signal(barrier, inc=1, device_id=z_device(zp(d)), device_id_type=MESH)
        pl.semaphore_signal(barrier, inc=1, device_id=item_peer(d), device_id_type=MESH)
    pl.semaphore_signal(barrier, inc=1, device_id=partner, device_id_type=MESH)
    load_i.start()
    load_u.start()
    load_w.start()
    load_c.start()
    load_p.start()
    load_i.wait()
    load_u.wait()
    pl.semaphore_wait(barrier, 7)

    sent = []

    def remote(src, dst, send, recv, device):
        copy = pltpu.make_async_remote_copy(
            src_ref=src, dst_ref=dst, send_sem=send, recv_sem=recv,
            device_id=device, device_id_type=MESH,
        )
        sent.append(copy)
        return copy

    mine_i = i_block(items, z, core)
    mine_u = users.at[pl.ds(u_at(0), ub)]
    relays = [remote(mine_i, mine_i, rl_send.at[0], rl_recv.at[0], partner)]
    relays[0].start()
    z_copies, u_copies = {}, {}
    for d in (1, 2, 3):
        z_copies[d] = remote(mine_i, mine_i, z_send.at[d], z_recv.at[d], z_device(zp(d)))
        z_copies[d].start()
    for d in (1, 3, 2):
        u_copies[d] = remote(mine_u, mine_u, u_send.at[d], u_recv.at[d], item_peer(d))
        u_copies[d].start()

    def relay(d):
        z_copies[d].wait_recv()
        block = i_block(items, zp(d), core)
        relays.append(remote(block, block, rl_send.at[d], rl_recv.at[d], partner))
        relays[-1].start()

    def i_rows(d, of_core):
        return pl.ds(pl.multiple_of((2 * zp(d) + of_core) * ib, ib), ib)

    own, other = core, 1 - core

    def take_items(d, of_core):
        at = i_rows(d, of_core)
        high, low = split(items[at, :])
        icat[at, 0:width] = high
        icat[at, width : 2 * width] = low
        icat[at, 2 * width : 3 * width] = high

    def take_users(d):
        at = pl.ds(u_at(d), ub)
        high, low = split(users[at, :])
        ucat[at, 0:width] = high
        ucat[at, width : 2 * width] = high
        ucat[at, 2 * width : 3 * width] = low

    def sum_squares(d):
        at = pl.ds(u_at(d), ub)
        sq[0, :, at] = jnp.sum(sq_part[at, :].T, axis=0, keepdims=True)

    scored = set()

    def score(d, *blocks):
        at = pl.ds(u_at(d), ub)
        both = jnp.concatenate([icat[i_rows(*block), :] for block in blocks], axis=0)
        predicted = lax.dot_general(
            ucat[at, :], both, (((1,), (1,)), ((), ())), preferred_element_type=F32
        )
        total = sq_part[at, :] if d in scored else jnp.zeros((ub, lane), F32)
        scored.add(d)
        for n, block in enumerate(blocks):
            col = i_rows(*block)
            weighted = conf[at, col] * (predicted[:, n * ib : (n + 1) * ib] - target[at, col])
            high, low = split(weighted)
            w_high[at, col] = high
            w_low[at, col] = low
            total = total + weighted * weighted
        sq_part[at, :] = total

    load_w.wait()
    load_c.wait()
    load_p.wait()
    tile = 128

    @pl.loop(0, rows // tile)
    def _(t):
        at = pl.ds(pl.multiple_of(t * tile, tile), tile)
        level = prefs[at, :]
        conf[at, :] = 2.0 + (2.0 * weight_ref[...]) * level.astype(F32)
        target[at, :] = jnp.where(level > 0, 1.0, 0.0).astype(F32)

    take_users(0)
    take_items(0, own)
    relay(1)
    take_items(1, own)
    relays[0].wait_recv()
    relays[1].wait_recv()
    take_items(0, other)
    take_items(1, other)
    near = ((0, own), (0, other), (1, own), (1, other))
    far_own, far_other = ((2, own), (3, own)), ((2, other), (3, other))
    score(0, *near)
    for d in (1, 2):
        u_copies[d].wait_recv()
        take_users(d)
        score(d, *near)
    relay(2)
    relay(3)
    take_items(2, own)
    take_items(3, own)
    for d in (0, 1, 2):
        score(d, *far_own)
    relays[2].wait_recv()
    relays[3].wait_recv()
    take_items(2, other)
    take_items(3, other)
    for d in (0, 1, 2):
        score(d, *far_other)
    for d in (0, 1, 2):
        sum_squares(d)
    u_copies[3].wait_recv()
    take_users(3)
    score(3, *near)
    score(3, *far_own)
    score(3, *far_other)
    sum_squares(3)

    sq_copies = []
    for d in (3, 1, 2):
        sq_copies.append(remote(sq.at[0], sq.at[d], sq_send.at[d], sq_recv.at[d], item_peer(d)))
        sq_copies[-1].start()

    g_copies = []

    def user_grads(*relations):
        for d in relations:
            at = pl.ds(u_at(d), ub)
            both = mm(w_high[at, :], icat[:, 0 : 2 * width])
            cross = mm(w_low[at, :], icat[:, 0:width])
            grad[at, :] = both[:, 0:width] + (both[:, width:] + cross)
        for d in relations:
            if d > 0:
                at = pl.ds(u_at(d), ub)
                copy = remote(
                    grad.at[at], grad_in.at[d - 1], gr_send.at[d], gr_recv.at[d], item_peer(d)
                )
                g_copies.append(copy)
                copy.start()

    for d in (3, 1, 2):
        user_grads(d)

    users_t[...] = users[...].T
    flat = users_t[...]
    user_sq = jnp.sum(flat * flat, axis=0, keepdims=True)
    for copy in sq_copies:
        copy.wait_recv()
    total_sq = sq[0]
    for d in (1, 2, 3):
        total_sq = total_sq + sq[d]
    bound_scale = 0.001 * jnp.sqrt(jnp.full((1, 1), float(cols * ni * width), F32))
    factor = jnp.minimum(
        1.0, clip_ref[...].astype(F32) * bound_scale / jnp.sqrt(total_sq * user_sq + 1e-06)
    )
    s_high, s_low = split(flat * factor)
    scat[0:width, :] = s_high
    scat[width:, :] = s_low

    pair_copies = {}

    def f_copy(k, c, src_z, to_z, slot):
        piece = pl.ds(c * iq, iq)
        return remote(
            pair_sum.at[src_z, piece], far_in.at[slot, piece],
            fr_send.at[k, c], fr_recv.at[slot, c], z_device(to_z),
        )

    def f_wait(slot, c):
        piece = far_in.at[slot, pl.ds(c * iq, iq)]
        pltpu.make_async_copy(piece, piece, fr_recv.at[slot, c]).wait()

    f_third = [f_copy(3, c, zp(3), zp(3), 3) for c in (0, 1)]

    def forward(d):
        to_z = zp(d)
        pair_copies[d].wait_recv()
        pair_sum[to_z] = i_block(part, to_z, core)[...] + pair_in[to_z]
        if d == 2:
            for c in (0, 1):
                f_copy(2, c, to_z, by_role(zp(1), zp(2)), 2).start()
        if d == 1:
            remote(
                pair_sum.at[to_z], far_in.at[1], fr_send.at[1, 0], fr_recv.at[1, 0], z_device(to_z)
            ).start()
        if d == 3:

            @pl.when(inner == 0)
            def _():
                for c in (0, 1):
                    f_third[c].start()

    def item_grads(pair):
        for d in pair:
            col = pl.ds(pl.multiple_of(zp(d) * big, big), big)
            both = mm(scat[...], w_high[:, col])
            cross = mm(scat[0:width, :], w_low[:, col])
            part[col, :] = (both[0:width] + (both[width:] + cross)).T
        for d in pair:
            to_z = zp(d)
            pair_copies[d] = remote(
                i_block(part, to_z, 1 - core), pair_in.at[to_z],
                pr_send.at[d], pr_recv.at[d], partner,
            )
            pair_copies[d].start()

    item_grads((2, 3, 1, 0))
    for d in (2, 3, 1, 0):
        forward(d)
    user_grads(0)

    @pl.when(inner == 1)
    def _():
        to_z = zp(3)
        for c in (0, 1):
            f_wait(2, c)
            piece = pl.ds(c * iq, iq)
            pair_sum[to_z, piece, :] = pair_sum[to_z, piece, :] + far_in[2, piece, :]
            f_third[c].start()

    for copy in g_copies:
        copy.wait_recv()
    user_grad = grad[pl.ds(u_at(0), ub), :]
    for d in (1, 2, 3):
        user_grad = user_grad + grad_in[d - 1]
    user_grad_ref[...] = user_grad

    pltpu.make_async_copy(far_in.at[1], far_in.at[1], fr_recv.at[1, 0]).wait()
    item_sum_ref[...] = pair_sum[z] + far_in[1]

    @pl.when(inner == 0)
    def _():
        for c in (0, 1):
            f_wait(2, c)
        item_sum_ref[...] = item_sum_ref[...] + far_in[2]

    for copy in sent:
        copy.wait_send()
    for c in (0, 1):
        f_wait(3, c)
    item_sum_ref[...] = item_sum_ref[...] + far_in[3]


def step_kernel(
    nu, ni,
    prefs_hbm, weight_hbm, clip_hbm, user_hbm, item_hbm,
    user_grad_ref, item_sum_ref,
    prefs, weight_ref, clip_ref, users, items, conf, target, ucat, icat, users_t, w_high, w_low,
    sq, sq_part, grad, grad_in, part, pair_in, pair_sum, far_in, scat,
    load_sem, ug_send, ug_recv, ig_send, ig_recv, rl_send, rl_recv,
    sq_send, sq_recv, gr_send, gr_recv, pr_send, pr_recv, fr_send, fr_recv,
):
    me_u, me_i = lax.axis_index("users"), lax.axis_index("items")
    half = nu // 2
    z, core = me_u // 2, me_u % 2
    partner = (2 * z + 1 - core, me_i)
    rows, cols = prefs.shape
    width = users.shape[1]
    ub, ib = rows // ni, cols // nu

    def u_slot(owner):
        return users.at[pl.ds(pl.multiple_of(owner * ub, ub), ub)]

    def i_slot(ref, owner):
        return ref.at[pl.ds(pl.multiple_of(owner * ib, ib), ib)]

    def item_peer(d):
        return (me_u, paired(me_i, d))

    def z_peer(d):
        return (2 * paired(z, d) + core, me_i)

    load_i = pltpu.make_async_copy(item_hbm, i_slot(items, me_u), load_sem.at[0])
    load_u = pltpu.make_async_copy(user_hbm, u_slot(me_i), load_sem.at[1])
    load_p = pltpu.make_async_copy(prefs_hbm, prefs, load_sem.at[2])
    load_w = pltpu.make_async_copy(weight_hbm, weight_ref, load_sem.at[3])
    load_c = pltpu.make_async_copy(clip_hbm, clip_ref, load_sem.at[4])
    load_i.start()
    load_u.start()
    load_w.start()
    load_c.start()
    load_p.start()

    barrier = pltpu.get_barrier_semaphore()
    for d in range(1, half):
        pl.semaphore_signal(barrier, inc=1, device_id=z_peer(d), device_id_type=MESH)
    for d in range(1, ni):
        pl.semaphore_signal(barrier, inc=1, device_id=item_peer(d), device_id_type=MESH)
    pl.semaphore_signal(barrier, inc=1, device_id=partner, device_id_type=MESH)
    load_i.wait()
    load_u.wait()
    pl.semaphore_wait(barrier, half + ni - 1)

    def remote(src, dst, send, recv, device):
        return pltpu.make_async_remote_copy(
            src_ref=src, dst_ref=dst, send_sem=send, recv_sem=recv,
            device_id=device, device_id_type=MESH,
        )

    mine_i = i_slot(items, me_u)
    mine_u = u_slot(me_i)
    z_copies, relays, u_copies = [], [], []
    relays.append(remote(mine_i, mine_i, rl_send.at[0], rl_recv.at[0], partner))
    relays[0].start()
    for d in range(1, half):
        z_copies.append(remote(mine_i, mine_i, ig_send.at[d], ig_recv.at[d], z_peer(d)))
        z_copies[-1].start()
    for d in range(1, ni):
        u_copies.append(remote(mine_u, mine_u, ug_send.at[d], ug_recv.at[d], item_peer(d)))
        u_copies[-1].start()

    load_w.wait()
    load_c.wait()
    load_p.wait()
    tile = min(rows, 128)

    @pl.loop(0, rows // tile)
    def _(t):
        at = pl.ds(pl.multiple_of(t * tile, tile), tile)
        level = prefs[at, :]
        conf[at, :] = 2.0 + (2.0 * weight_ref[...]) * level.astype(F32)
        target[at, :] = jnp.where(level > 0, 1.0, 0.0).astype(F32)

    big, lane = 256, 128

    def relay(d):
        z_copies[d - 1].wait_recv()
        block = i_slot(items, 2 * paired(z, d) + core)
        relays.append(remote(block, block, rl_send.at[d], rl_recv.at[d], partner))
        relays[-1].start()

    def take_items(start, size):
        at = pl.ds(start, size)
        high, low = split(items[at, :])
        icat[at, 0:width] = high
        icat[at, width : 2 * width] = low
        icat[at, 2 * width : 3 * width] = high

    def take_users(start, size):
        at = pl.ds(start, size)
        high, low = split(users[at, :])
        ucat[at, 0:width] = high
        ucat[at, width : 2 * width] = high
        ucat[at, 2 * width : 3 * width] = low

    def score(row, height, start, extent, first):
        at = pl.ds(row, height)
        left = ucat[at, :]
        total = jnp.zeros((height, lane), F32) if first else sq_part[at, :]
        for k in range(extent // big):
            col = pl.ds(start + k * big, big)
            predicted = lax.dot_general(
                left, icat[col, :], (((1,), (1,)), ((), ())), preferred_element_type=F32
            )
            weighted = conf[at, col] * (predicted - target[at, col])
            high, low = split(weighted)
            w_high[at, col] = high
            w_low[at, col] = low
            square = weighted * weighted
            for m in range(big // lane):
                total = total + square[:, m * lane : (m + 1) * lane]
        sq_part[at, :] = total

    if half == 4 and ni == 4 and ub == big and cols == 4 * big:
        near = pl.multiple_of(z // 2 * (2 * big), 2 * big)

        def i_at(d):
            return pl.multiple_of(paired(z, d) * big, big)

        def u_at(d):
            return pl.multiple_of(paired(me_i, d) * ub, ub)

        relay(1)
        take_users(u_at(0), ub)
        relays[0].wait_recv()
        relays[1].wait_recv()
        take_items(near, 2 * big)
        score(u_at(0), ub, near, 2 * big, True)
        for d in (1, 2):
            u_copies[d - 1].wait_recv()
            take_users(u_at(d), ub)
            score(u_at(d), ub, near, 2 * big, True)
        relay(2)
        relay(3)
        u_copies[2].wait_recv()
        take_users(u_at(3), ub)
        score(u_at(3), ub, near, 2 * big, True)
        for d in (2, 3):
            relays[d].wait_recv()
            take_items(i_at(d), big)
            for t in range(ni):
                score(t * big, big, i_at(d), big, False)
        sq[0] = jnp.sum(sq_part[...].T, axis=0, keepdims=True)
    else:
        for d in range(1, half):
            relay(d)
        for copy in u_copies + relays:
            copy.wait_recv()
        take_items(0, cols)
        take_users(0, rows)

        @pl.loop(0, rows // big)
        def _(t):
            score(pl.multiple_of(t * big, big), big, 0, cols, True)

        sq[0] = jnp.sum(sq_part[...].T, axis=0, keepdims=True)

    sq_copies = []
    for d in range(1, ni):
        sq_copies.append(remote(sq.at[0], sq.at[d], sq_send.at[d], sq_recv.at[d], item_peer(d)))
        sq_copies[-1].start()

    g_copies = []
    for d in list(range(1, ni)) + [0]:
        owner = paired(me_i, d)
        at = pl.ds(pl.multiple_of(owner * ub, ub), ub)
        both = mm(w_high[at, :], icat[:, 0 : 2 * width])
        cross = mm(w_low[at, :], icat[:, 0:width])
        grad[at, :] = both[:, 0:width] + (both[:, width:] + cross)
        if d > 0:
            g_copies.append(
                remote(grad.at[at], grad_in.at[d - 1], gr_send.at[d], gr_recv.at[d], item_peer(d))
            )
            g_copies[-1].start()

    users_t[...] = users[...].T
    flat = users_t[...]
    user_sq = jnp.sum(flat * flat, axis=0, keepdims=True)
    for copy in sq_copies:
        copy.wait_recv()
    total_sq = sq[0]
    for d in range(1, ni):
        total_sq = total_sq + sq[d]
    bound_scale = 0.001 * jnp.sqrt(jnp.full((1, 1), float(cols * ni * width), F32))
    factor = jnp.minimum(
        1.0, clip_ref[...].astype(F32) * bound_scale / jnp.sqrt(total_sq * user_sq + 1e-06)
    )
    s_high, s_low = split(flat * factor)
    scat[0:width, :] = s_high
    scat[width:, :] = s_low

    chunk = max(2 * ib, min(256, cols))
    groups = cols // chunk
    per = half // groups
    my_group = z // per
    pair_copies, far_copies = {}, {}

    def relations(order):
        return [(groups - order) * per + e for e in range(per)]

    def forward(order):
        for d in relations(order):
            to_z = paired(z, d)
            pair_copies[d].wait_recv()
            pair_sum[to_z] = i_slot(part, 2 * to_z + core)[...] + pair_in[to_z]
            if d > 0:
                far_copies[d] = remote(
                    pair_sum.at[to_z], far_in.at[d], fr_send.at[d], fr_recv.at[d], z_peer(d)
                )
                far_copies[d].start()

    for order in range(1, groups + 1):
        group = paired(my_group, groups - order)
        col = pl.ds(pl.multiple_of(group * chunk, chunk), chunk)
        both = mm(scat[...], w_high[:, col])
        cross = mm(scat[0:width, :], w_low[:, col])
        part[col, :] = (both[0:width] + (both[width:] + cross)).T
        for d in relations(order):
            to_z = paired(z, d)
            pair_copies[d] = remote(
                i_slot(part, 2 * to_z + 1 - core), pair_in.at[to_z],
                pr_send.at[d], pr_recv.at[d], partner,
            )
            pair_copies[d].start()
        if order > 1:
            forward(order - 1)
    forward(groups)

    for copy in g_copies:
        copy.wait_recv()
    user_grad = grad[pl.ds(pl.multiple_of(me_i * ub, ub), ub), :]
    for d in range(1, ni):
        user_grad = user_grad + grad_in[d - 1]
    user_grad_ref[...] = user_grad

    sent = z_copies + relays + u_copies + sq_copies + g_copies + list(pair_copies.values())
    for copy in sent + list(far_copies.values()):
        copy.wait_send()
    item_sum = pair_sum[z]
    for d in range(1, half):
        far_copies[d].wait_recv()
        item_sum = item_sum + far_in[d]
    item_sum_ref[...] = item_sum


def update_kernel(
    user_grad, item_sum, user_emb, user_acc, item_emb, item_acc, noise,
    new_user_emb, new_user_acc, new_item_emb, new_item_acc,
):
    grad = user_grad[...]
    acc = user_acc[...] + grad * grad
    new_user_acc[...] = acc
    new_user_emb[...] = user_emb[...] - learn_rate * grad / jnp.sqrt(acc)
    grad = item_sum[...] + noise_step * noise[...].astype(F32)
    acc = item_acc[...] + grad * grad
    new_item_acc[...] = acc
    new_item_emb[...] = item_emb[...] - learn_rate * grad / jnp.sqrt(acc)


def local(prefs, item_weight, clip_units, user_emb, user_acc, item_emb, item_acc, noise):
    nu, ni = lax.axis_size("users"), lax.axis_size("items")
    rows, cols = prefs.shape
    ub, width = user_emb.shape
    ib = item_emb.shape[0]
    half = nu // 2
    vmem = pl.BlockSpec(memory_space=pltpu.VMEM)
    hbm = pl.BlockSpec(memory_space=pltpu.HBM)
    dma = pltpu.SemaphoreType.DMA
    line = nu == 8 and ni == 4 and ub == 256 and ib == 128 and width == 128
    if line:
        kernel = line_kernel
        semaphores = [
            dma((5,)),
            dma((4,)), dma((4,)),
            dma((4,)), dma((4,)),
            dma((4,)), dma((4,)),
            dma((4,)), dma((4,)),
            dma((4,)), dma((4,)),
            dma((4,)), dma((4,)),
            dma((4, 2)), dma((4, 2)),
        ]
    else:
        kernel = functools.partial(step_kernel, nu, ni)
        semaphores = [
            dma((5,)),
            dma((ni,)), dma((ni,)),
            dma((half,)), dma((half,)),
            dma((half,)), dma((half,)),
            dma((ni,)), dma((ni,)),
            dma((ni + 1,)), dma((ni + 1,)),
            dma((half,)), dma((half,)),
            dma((half,)), dma((half,)),
        ]
    user_grad, item_sum = pl.pallas_call(
        kernel,
        out_shape=(
            jax.ShapeDtypeStruct((ub, width), F32),
            jax.ShapeDtypeStruct((ib, width), F32),
        ),
        in_specs=[hbm] * 5,
        out_specs=(vmem, vmem),
        scratch_shapes=[
            pltpu.VMEM((rows, cols), jnp.int32),
            pltpu.VMEM((1, cols), F32),
            pltpu.VMEM((1, rows), jnp.int32),
            pltpu.VMEM((rows, width), F32),
            pltpu.VMEM((cols, width), F32),
            pltpu.VMEM((rows, cols), F32),
            pltpu.VMEM((rows, cols), F32),
            pltpu.VMEM((rows, 3 * width), BF16),
            pltpu.VMEM((cols, 3 * width), BF16),
            pltpu.VMEM((width, rows), F32),
            pltpu.VMEM((rows, cols), BF16),
            pltpu.VMEM((rows, cols), BF16),
            pltpu.VMEM((ni, 1, rows), F32),
            pltpu.VMEM((rows, 128), F32),
            pltpu.VMEM((rows, width), F32),
            pltpu.VMEM((ni - 1, ub, width), F32),
            pltpu.VMEM((cols, width), F32),
            pltpu.VMEM((half, ib, width), F32),
            pltpu.VMEM((half, ib, width), F32),
            pltpu.VMEM((half, ib, width), F32),
            pltpu.VMEM((2 * width, rows), BF16),
        ] + semaphores,
        compiler_params=pltpu.CompilerParams(
            collective_id=0, has_side_effects=True, vmem_limit_bytes=48 * 1024 * 1024
        ),
    )(*[pltpu.with_memory_space_constraint(x, pltpu.HBM) for x in (prefs, item_weight[None, :], clip_units[None, :], user_emb, item_emb)])
    user_shape = jax.ShapeDtypeStruct((ub, width), F32)
    item_shape = jax.ShapeDtypeStruct((ib, width), F32)
    vmem = pl.BlockSpec(memory_space=pltpu.VMEM)
    return pl.pallas_call(
        update_kernel,
        out_shape=(user_shape, user_shape, item_shape, item_shape),
        in_specs=[vmem] * 7,
        out_specs=(vmem,) * 4,
        compiler_params=pltpu.CompilerParams(vmem_limit_bytes=4 * 1024 * 1024),
    )(user_grad, item_sum, user_emb, user_acc, item_emb, item_acc, noise)


def solution(mesh):
    placed = (
        P("users", "items"),
        P("items"),
        P("users"),
        P(("users", "items"), None),
        P(("users", "items"), None),
        P(("items", "users"), None),
        P(("items", "users"), None),
        P(("items", "users"), None),
    )
    return jax.shard_map(
        local,
        mesh=mesh,
        in_specs=placed,
        out_specs=(
            P(("users", "items"), None),
            P(("users", "items"), None),
            P(("items", "users"), None),
            P(("items", "users"), None),
        ),
        check_vma=False,
    )
```
